256 devices in a mesh: kv: 4 (over x), seq: 64 (over z, y, core).
Axes of the slice: x: 4, y: 4, z: 8, core: 2. Of those that a mesh axis runs over, the one named last changes fastest.
Arguments:
- queries: bfloat16 [8192, 12288], P('seq', 'kv'), may hold values from -400 to 400
- cache_keys: bfloat16 [65536, 768], P('seq', 'kv'), may hold values from -6 to 6
- cache_values: bfloat16 [65536, 512], P('seq', 'kv'), may hold values from -6 to 6
- incoming_keys: bfloat16 [8192, 768], P('seq', 'kv'), may hold values from -6 to 6
- new_values: bfloat16 [8192, 512], P('seq', 'kv'), may hold values from -6 to 6
- comp_key_weight: bfloat16 [6144, 192], P('kv'), may hold values from -0.078125 to 0.078125
- comp_value_weight: bfloat16 [4096, 128], P('kv'), may hold values from -0.09375 to 0.09375
- select_blocks: int32 [256, 4, 16], P('seq', 'kv'), may hold values from 0 to 1023, as said below
- gate_weight: bfloat16 [64, 192, 3], P('kv'), may hold values from -0.4375 to 0.4375
Outputs:
- attended: bfloat16 [8192, 8192], P('seq', 'kv')
The draws below stay inside these ranges and needn't reach their ends.
Inputs may be any that keep to these rules, and one draw needn't show every extreme that they name: `select_blocks`: each row names 16 different blocks. For each KV group, the rows of one device of seq (4 tiles) name blocks of any one cache shard (the 16 blocks of one index of seq) at most 2 times in all, and in every draw the rows of every device name one shard's blocks exactly 2 times.
All inputs are finite; a program needn't handle non-finite values.
Results may differ from the reference program's by a relative error of at most 0.012.
Values may be sent and summed in bfloat16 or wider, within the bound.
No kernel may reach another device: no remote copies, remote signals or barrier semaphores. Data moves between devices by JAX's collectives and lax.ppermute only.
A program may use at most 128 MiB of HBM per device.

```python
import jax
import jax.numpy as jnp
from jax import lax

HEADS = 64
KV_GROUPS = 4
HEAD_QK = 192
HEAD_V = 128
CMP_STRIDE = 16
SEL_BLOCK = 64
TOPN = 16
WINDOW = 512
TILE = 32
Q_DEV = 128
QUERIES = 8192
CACHE = 65536
TILES_DEV = 4
BLK_DEV = 16
CAP = 2
N_SEQ = 64


def draw_queries(key, part):
    drawn = jax.random.normal(jax.random.fold_in(key, 11), (QUERIES, HEADS * HEAD_QK), jnp.float32) * 2.5
    return jnp.clip(drawn, -400.0, 400.0).astype(jnp.bfloat16)


def one_device(subkey, busy):
    picks = TILES_DEV * TOPN
    slots = N_SEQ * CAP
    key_score, key_offset, key_order = jax.random.split(subkey, 3)
    places = jnp.arange(slots, dtype=jnp.int32)
    pool = places // CAP
    score = jax.random.randint(key_score, (slots,), 0, 1 << 16, dtype=jnp.int32) * slots + places
    score = jnp.where(pool == busy, places - slots, score)
    owner = pool[jnp.argsort(score, stable=True)][:picks]
    owner = owner[jax.random.permutation(key_order, picks)].reshape(TILES_DEV, TOPN)
    onehot = (owner[:, :, None] == jnp.arange(N_SEQ, dtype=jnp.int32)[None, None, :]).astype(jnp.int32)
    ranking = jnp.sum((jnp.cumsum(onehot, axis=1) - 1) * onehot, axis=2)
    offset = jax.random.randint(key_offset, (TILES_DEV, N_SEQ), 0, BLK_DEV, dtype=jnp.int32)
    local = (jnp.take_along_axis(offset, owner, axis=1) + ranking) % BLK_DEV
    return owner * BLK_DEV + local


def draw_select_blocks(key, part):
    columns = []
    for group in range(KV_GROUPS):
        group_key = jax.random.fold_in(key, 101 + group)
        busy = jax.random.randint(jax.random.fold_in(group_key, 7), (), 0, N_SEQ, dtype=jnp.int32)
        subkeys = jax.random.split(jax.random.fold_in(group_key, 9), N_SEQ)
        chosen = jax.vmap(lambda subkey: one_device(subkey, busy))(subkeys)
        columns.append(chosen.reshape(N_SEQ * TILES_DEV, TOPN))
    return jnp.stack(columns, axis=1).astype(jnp.int32)


def shard_levels(key, extent, cuts, least, top_value):
    def one(dim, shards_of):
        heights = jax.random.uniform(jax.random.fold_in(jax.random.fold_in(key, 6), dim), (shards_of,), jnp.float32, least / len(cuts), top_value / len(cuts))
        return jnp.repeat(jnp.exp(heights), extent[dim] // shards_of).reshape((-1,) + (1,) * (len(extent) - dim - 1))

    level = one(*cuts[0])
    for cut in cuts[1:]:
        level = level * one(*cut)
    return level


def normal_values(rng, dims, scale, limit, cuts=(), kind=jnp.bfloat16):
    gain = shard_levels(rng, dims, cuts, -0.22, 0.18) if cuts else 1.0
    result = jax.random.normal(rng, dims, jnp.float32) * scale * gain
    return jnp.minimum(jnp.maximum(result, -limit), limit).astype(kind)


def setup_inputs(seed: int = 0) -> dict:
    key_list = jax.random.split(jax.random.key(seed), 10)
    queries = draw_queries(jax.random.fold_in(key_list[9], 71), 0)
    cache_keys = normal_values(key_list[1], (CACHE, KV_GROUPS * HEAD_QK), 1.0, 6.0, ((0, 64), (1, 4)))
    cache_values = normal_values(key_list[2], (CACHE, KV_GROUPS * HEAD_V), 1.0, 6.0, ((0, 64), (1, 4)))
    incoming_keys = normal_values(key_list[3], (QUERIES, KV_GROUPS * HEAD_QK), 1.0, 6.0, ((0, 64), (1, 4)))
    new_values = normal_values(key_list[4], (QUERIES, KV_GROUPS * HEAD_V), 1.0, 6.0, ((0, 64), (1, 4)))
    comp_key_weight = normal_values(key_list[5], (2 * CMP_STRIDE * HEAD_QK, HEAD_QK), (2 * CMP_STRIDE * HEAD_QK) ** -0.5, 0.078125, ((0, 4),))
    comp_value_weight = normal_values(key_list[6], (2 * CMP_STRIDE * HEAD_V, HEAD_V), (2 * CMP_STRIDE * HEAD_V) ** -0.5, 0.09375, ((0, 4),))
    select_blocks = draw_select_blocks(jax.random.fold_in(key_list[9], 71), 0)
    gate_weight = normal_values(key_list[8], (HEADS, HEAD_QK, 3), HEAD_QK ** -0.5, 0.4375, ((0, 4),))
    return {"queries": queries, "cache_keys": cache_keys, "cache_values": cache_values, "incoming_keys": incoming_keys, "new_values": new_values, "comp_key_weight": comp_key_weight, "comp_value_weight": comp_value_weight, "select_blocks": select_blocks, "gate_weight": gate_weight}


MASKED = -1e30


def attend(rows, keys, values, allowed):
    scale = keys.shape[-1] ** -0.5
    scores = jnp.dot(rows, keys.T, preferred_element_type=jnp.float32) * scale
    scores = jnp.where(allowed, scores, MASKED)
    top = jnp.max(scores, axis=-1, keepdims=True)
    weights = jnp.exp(scores - top)
    total = jnp.sum(weights, axis=-1, keepdims=True)
    mixed = jnp.dot(weights.astype(jnp.bfloat16), values, preferred_element_type=jnp.float32)
    return mixed / total


def reference(queries, cache_keys, cache_values, incoming_keys, new_values, comp_key_weight, comp_value_weight, select_blocks, gate_weight):
    per_group = HEADS // KV_GROUPS
    count = CACHE // CMP_STRIDE - 1
    half_keys = CMP_STRIDE * HEAD_QK
    half_values = CMP_STRIDE * HEAD_V
    split_queries = queries.reshape(QUERIES, KV_GROUPS, per_group, HEAD_QK)
    span = Q_DEV + WINDOW
    offsets = jnp.arange(span, dtype=jnp.int32)[None, :] - jnp.arange(Q_DEV, dtype=jnp.int32)[:, None]
    near_rows = jnp.repeat((offsets > 0) & (offsets <= WINDOW), per_group, axis=0)
    results = []
    for group in range(KV_GROUPS):
        keys = cache_keys[:, group * HEAD_QK:(group + 1) * HEAD_QK]
        values = cache_values[:, group * HEAD_V:(group + 1) * HEAD_V]
        fresh_keys = incoming_keys[:, group * HEAD_QK:(group + 1) * HEAD_QK]
        fresh_values = new_values[:, group * HEAD_V:(group + 1) * HEAD_V]
        comp_keys = (jnp.dot(keys[:CACHE - CMP_STRIDE].reshape(count, half_keys), comp_key_weight[:half_keys], preferred_element_type=jnp.float32)
                     + jnp.dot(keys[CMP_STRIDE:].reshape(count, half_keys), comp_key_weight[half_keys:], preferred_element_type=jnp.float32)).astype(jnp.bfloat16)
        comp_values = (jnp.dot(values[:CACHE - CMP_STRIDE].reshape(count, half_values), comp_value_weight[:half_values], preferred_element_type=jnp.float32)
                       + jnp.dot(values[CMP_STRIDE:].reshape(count, half_values), comp_value_weight[half_values:], preferred_element_type=jnp.float32)).astype(jnp.bfloat16)
        group_queries = split_queries[:, group]
        blocks = group_queries.reshape(N_SEQ, Q_DEV * per_group, HEAD_QK)
        compressed_out = lax.map(lambda block: attend(block, comp_keys, comp_values, True), blocks)
        key_blocks = keys.reshape(CACHE // SEL_BLOCK, SEL_BLOCK, HEAD_QK)
        value_block_list = values.reshape(CACHE // SEL_BLOCK, SEL_BLOCK, HEAD_V)
        tiles = group_queries.reshape(QUERIES // TILE, TILE * per_group, HEAD_QK)

        def pick(inputs):
            tile, chosen = inputs
            chosen_keys = key_blocks[chosen].reshape(TOPN * SEL_BLOCK, HEAD_QK)
            chosen_values = value_block_list[chosen].reshape(TOPN * SEL_BLOCK, HEAD_V)
            return attend(tile, chosen_keys, chosen_values, True)

        selected_out = lax.map(pick, (tiles, select_blocks[:, group]))
        joined_keys = jnp.concatenate([keys[CACHE - WINDOW:], fresh_keys])
        joined_values = jnp.concatenate([values[CACHE - WINDOW:], fresh_values])

        def slide(inputs):
            index, block = inputs
            start = (index * Q_DEV).astype(jnp.int32)
            window_keys = lax.dynamic_slice_in_dim(joined_keys, start, span, 0)
            window_values = lax.dynamic_slice_in_dim(joined_values, start, span, 0)
            return attend(block, window_keys, window_values, near_rows)

        window_out = lax.map(slide, (jnp.arange(N_SEQ, dtype=jnp.int32), blocks))
        results.append((compressed_out.reshape(QUERIES, per_group, HEAD_V),
                        selected_out.reshape(QUERIES, per_group, HEAD_V),
                        window_out.reshape(QUERIES, per_group, HEAD_V)))
    compressed_all = jnp.concatenate([item[0] for item in results], axis=1)
    selected_all = jnp.concatenate([item[1] for item in results], axis=1)
    window_all = jnp.concatenate([item[2] for item in results], axis=1)
    logits = jnp.einsum("thd,hdb->thb", queries.reshape(QUERIES, HEADS, HEAD_QK).astype(jnp.float32), gate_weight.astype(jnp.float32))
    gates = jax.nn.sigmoid(logits)
    mixed = gates[:, :, 0:1] * compressed_all + gates[:, :, 1:2] * selected_all + gates[:, :, 2:3] * window_all
    return mixed.astype(jnp.bfloat16).reshape(QUERIES, HEADS * HEAD_V)
```

```python
import functools
import math

import jax
import jax.numpy as jnp
from jax import lax
from jax.experimental import pallas as pl
from jax.experimental.pallas import tpu as pltpu
from jax.sharding import Mesh, PartitionSpec as P


BLOCK = 64
ROWS = 160
WINDOW = 512
MASKED = -1e30
BF = jnp.bfloat16
F32 = jnp.float32
Z, Y, C = 8, 4, 2


def pack(keys, values):
    k = keys.reshape(-1, BLOCK, keys.shape[1])
    v = values.reshape(-1, BLOCK, values.shape[1])
    high = jnp.concatenate([k[:, :32, 128:], k[:, 32:, 128:]], axis=2)
    return jnp.concatenate([v, k[:, :, :128], high], axis=1)


def nt_dot(a, b):
    return lax.dot_general(a, b, (((1,), (1,)), ((), ())), preferred_element_type=F32)


def stage(n, coef, score, value, ahead, now, finish):
    peak = acc = None
    at = 0
    for j in range(n):
        v = value(0 if now is None else now[0], j)
        w = v.shape[0]
        if ahead is not None:
            g, s_ref, m_ref = ahead
            s = score(g, j)
            s_ref[:, at : at + w] = s
            for k in range(0, w, 128):
                piece = s[:, k : k + 128]
                peak = piece if peak is None else jnp.maximum(peak, piece)
        if now is not None:
            g, s_ref, m_ref = now
            top = m_ref[...]
            p = [
                jnp.exp2(s_ref[:, k : k + 128] * coef - top).astype(BF)
                for k in range(at, at + w, 128)
            ]
            both = jnp.concatenate([v, jnp.ones_like(v)], axis=1)
            part = jnp.dot(jnp.concatenate(p, axis=1), both, preferred_element_type=F32)
            acc = part if acc is None else acc + part
        at += w
    if ahead is not None:
        m_ref = ahead[2]
        peak = jnp.max(peak, axis=1, keepdims=True) * coef
        m_ref[...] = jnp.broadcast_to(peak, m_ref.shape)
    if now is not None:
        finish(now[0], acc[:, :128] / acc[:, 128:])


def attend_groups(groups, n, coef, score, value, finish, ready, refs):
    sa, sb, ma, mb = refs
    ready(0)
    stage(n, coef, score, value, (0, sa, ma), None, finish)

    def body(i, carry):
        ready(2 * i + 1)
        stage(n, coef, score, value, (2 * i + 1, sb, mb), (2 * i, sa, ma), finish)

        @pl.when(2 * i + 2 < groups)
        def _():
            ready(2 * i + 2)
            stage(n, coef, score, value, (2 * i + 2, sa, ma), (2 * i + 1, sb, mb), finish)

        @pl.when(2 * i + 2 >= groups)
        def _():
            stage(n, coef, score, value, None, (2 * i + 1, sb, mb), finish)

        return carry

    lax.fori_loop(0, groups // 2, body, 0)


def score_scratch(rows, keys):
    return [pltpu.VMEM((rows, keys), F32)] * 2 + [pltpu.VMEM((rows, 128), F32)] * 2


def query_kernel(q_ref, g_ref, qa_ref, qb_ref, gate_ref):
    for h in range(qa_ref.shape[0]):
        x = q_ref[:, 192 * h : 192 * h + 192]
        zero = jnp.zeros((x.shape[0], 64), BF)
        qa = jnp.concatenate([x, zero], axis=1)
        qa_ref[h] = qa
        qb_ref[h] = jnp.concatenate([x[:, :128], zero, x[:, 128:]], axis=1)
        gate_ref[h] = jax.nn.sigmoid(nt_dot(qa, g_ref[h]))


def query_layout(queries, g):
    heads, t = g.shape[0], queries.shape[0]
    shape = jax.ShapeDtypeStruct((heads, t, 256), BF)
    return pl.pallas_call(
        query_kernel,
        out_shape=(shape, shape, jax.ShapeDtypeStruct((heads, t, 8), F32)),
        cost_estimate=pl.CostEstimate(flops=0, bytes_accessed=4 << 20, transcendentals=0),
        name="query_layout",
    )(queries, g)


def gather_kernel(plan, first, rq, *refs):
    srcs, (out_ref, buf, sem, out_sem) = refs[:-4], refs[-4:]
    width = len(plan)
    inward, outward = [], []
    for dest in range(Y * C):
        for s, (src, base) in enumerate(plan):
            i = dest * width + s
            copy = pltpu.make_async_copy(
                srcs[src].at[base + rq[dest, first + s]], buf.at[i], sem.at[i]
            )
            copy.start()
            inward.append(copy)
    for dest in range(Y * C):
        for copy in inward[dest * width : (dest + 1) * width]:
            copy.wait()
        span = pl.ds(dest * width, width)
        copy = pltpu.make_async_copy(buf.at[span], out_ref.at[span], out_sem.at[dest])
        copy.start()
        outward.append(copy)
    for copy in outward:
        copy.wait()


def gather_blocks(srcs, plan, first, rq):
    count = Y * C * len(plan)
    return pl.pallas_call(
        functools.partial(gather_kernel, plan, first),
        grid_spec=pltpu.PrefetchScalarGridSpec(
            num_scalar_prefetch=1,
            grid=(1,),
            in_specs=[pl.BlockSpec(memory_space=pl.ANY)] * len(srcs),
            out_specs=pl.BlockSpec(memory_space=pl.ANY),
            scratch_shapes=[
                pltpu.VMEM((count, ROWS, 128), BF),
                pltpu.SemaphoreType.DMA((count,)),
                pltpu.SemaphoreType.DMA((Y * C,)),
            ],
        ),
        out_shape=jax.ShapeDtypeStruct((count, ROWS, 128), BF),
        cost_estimate=pl.CostEstimate(
            flops=0, bytes_accessed=count * ROWS * 128 * 4, transcendentals=0
        ),
        name="gather_blocks",
    )(rq, *srcs)


def weight_kernel(info, k_ref, v_ref, both_ref, half_ref):
    c = info[0]
    for h in range(2):
        for j in range(6):
            x = k_ref[:, 768 * h + 128 * j : 768 * h + 128 * j + 128]
            both_ref[h, 192 * j : 192 * j + 192, :] = x
        both_ref[h, 1152:1664, :] = v_ref[512 * h : 512 * h + 512, :]
    half_ref[...] = both_ref[c]


def weight_pack(info, wk, wv):
    whole = lambda a: pl.BlockSpec(a.shape, lambda i, c: (0, 0))
    return pl.pallas_call(
        weight_kernel,
        grid_spec=pltpu.PrefetchScalarGridSpec(
            num_scalar_prefetch=1,
            grid=(1,),
            in_specs=[whole(wk), whole(wv)],
            out_specs=(
                pl.BlockSpec((2, 1664, 128), lambda i, c: (0, 0, 0)),
                pl.BlockSpec((1664, 128), lambda i, c: (0, 0)),
            ),
        ),
        out_shape=(
            jax.ShapeDtypeStruct((2, 1664, 128), BF),
            jax.ShapeDtypeStruct((1664, 128), BF),
        ),
        cost_estimate=pl.CostEstimate(flops=0, bytes_accessed=3 << 20, transcendentals=0),
        name="weight_pack",
    )(info, wk, wv)


def compress_kernel(
    info, xk_ref, xv_ref, ek_ref, ev_ref, own_ref, m1_ref, m2_ref, o1_ref, o2_ref, out_ref
):
    c, x = info[0], info[1]
    row = lax.broadcasted_iota(jnp.int32, (64, 1), 0)

    def taken(ref, edge, start, width, first):
        span = pl.ds(start, width)
        a = ref[:, span].astype(F32)
        lead = jnp.where(row == 0, edge[:, span].astype(F32), jnp.roll(a, 1, axis=0))
        return jnp.where(first, lead, a).astype(BF)

    step = 1 - 2 * c
    near, far, across = (x - step) & 3, (x + step) & 3, (x + 2) & 3
    pieces = [(own_ref.at[h], x, h) for h in range(2)]
    pieces += [(m1_ref.at[h], near, h) for h in range(2)]
    pieces += [(o1_ref.at[h], far, h) for h in range(2)]
    pieces += [(m2_ref, across, c), (o2_ref, across, 1 - c)]
    keys = jnp.zeros((64, 192), F32)
    values = jnp.zeros((64, 128), F32)
    for ref, i, h in pieces:
        at = 8 * (i & 1) + 4 * h
        a = taken(xk_ref, ek_ref, pl.multiple_of(at * 192, 256), 768, i < 2)
        for j in range(3):
            w = jnp.concatenate(
                [ref[384 * j : 384 * j + 192, :], ref[384 * j + 192 : 384 * j + 384, :]], axis=1
            )
            keys = keys + nt_dot(a[:, 256 * j : 256 * j + 256], w)
        a = taken(xv_ref, ev_ref, pl.multiple_of(at * 128, 512), 512, i < 2)
        values = values + jnp.dot(a, ref[1152:1664, :], preferred_element_type=F32)
    keys = keys.astype(BF)
    out_ref[0, 0:64, :] = values.astype(BF)
    out_ref[0, 64:128, :] = keys[:, :128]
    out_ref[0, 128:160, :] = jnp.concatenate([keys[:32, 128:], keys[32:, 128:]], axis=1)


def compress(info, *args):
    full = lambda a: pl.BlockSpec(a.shape, lambda i, c, n=a.ndim: (0,) * n)
    return pl.pallas_call(
        compress_kernel,
        grid_spec=pltpu.PrefetchScalarGridSpec(
            num_scalar_prefetch=1,
            grid=(1,),
            in_specs=[full(a) for a in args],
            out_specs=pl.BlockSpec((1, ROWS, 128), lambda i, c: (0, 0, 0)),
        ),
        out_shape=jax.ShapeDtypeStruct((1, ROWS, 128), BF),
        cost_estimate=pl.CostEstimate(
            flops=2 * 64 * (6144 * 192 + 4096 * 128), bytes_accessed=4 << 20, transcendentals=0
        ),
        name="compress",
    )(info, *args)


HB = 4


def part_of(ref, first, count, part):
    n = count * 32
    blocks = pl.ds(first, count)
    low = ref[blocks, 64 + 32 * part : 96 + 32 * part, :].reshape(n, 128)
    high = ref[blocks, 128:160, :].reshape(n, 128)
    return jnp.concatenate([low, high], axis=1)


def values_of(ref, first, count, part):
    return ref[pl.ds(first, count), 32 * part : 32 * part + 32, :].reshape(count * 32, 128)


def nothing(g):
    pass


def window_kernel(coef, core, qa_ref, qb_ref, g_ref, wm_ref, wt_ref, own_ref, out_ref, bias, *refs):
    c = core[0]
    t = qa_ref.shape[1]
    rows = HB * t
    plan = ((wm_ref, -256 - 256 * c, c), (wt_ref, -512 + 256 * c, 1 - c), (own_ref, 0, c))
    at = lax.broadcasted_iota(jnp.int32, (t, 1), 0) + c * t
    for part in range(2):
        for k, (ref, base, ring) in enumerate(plan):
            i = lax.broadcasted_iota(jnp.int32, (1, 128), 1)
            which = lax.shift_right_logical(i, 6)
            which = which + ring - 2 * which * ring
            where = base + which * t + (lax.shift_right_logical(i, 5) & 1) * 64 + part * 32
            where = where + (i & 31)
            ok = (where <= at) & (where > at - WINDOW)
            bias[part, :, 128 * k : 128 * k + 128] = jnp.where(ok, 0.0, MASKED)

    def score(g, j):
        q = (qa_ref, qb_ref)[j][pl.ds(g * HB, HB)].reshape(rows, 256)
        k = jnp.concatenate([part_of(ref, 0, 4, j) for ref, _, _ in plan], axis=0)
        s = nt_dot(q, k).reshape(HB, t, 384) + bias[j][None]
        return s.reshape(rows, 384)

    def value(g, j):
        return jnp.concatenate([values_of(ref, 0, 4, j) for ref, _, _ in plan], axis=0)

    def finish(g, out):
        for h in range(HB):
            sl = pl.ds(pl.multiple_of((g * HB + h) * 128, 128), 128)
            out_ref[:, sl] = out[h * t : (h + 1) * t] * g_ref[g * HB + h, :, 2:3]

    attend_groups(qa_ref.shape[0] // HB, 2, coef, score, value, finish, nothing, refs)


def compressed_kernel(
    coef, hole, qa_ref, qb_ref, g_ref, plane_ref, mine_ref, other_ref, add_ref, out_ref, *refs
):
    t = qa_ref.shape[1]
    rows = HB * t
    plan = []
    for kind, ref in enumerate((plane_ref, mine_ref, other_ref)):
        for first in range(0, ref.shape[0], 16):
            for part in range(2):
                plan.append((kind, ref, first, min(16, ref.shape[0] - first), part))

    def score(g, j):
        kind, ref, first, count, part = plan[j]
        q = (qa_ref, qb_ref)[part][pl.ds(g * HB, HB)].reshape(rows, 256)
        s = nt_dot(q, part_of(ref, first, count, part))
        if part == 0:
            col = lax.broadcasted_iota(jnp.int32, (1, count * 32), 1) + first * 32
            s = jnp.where((col == hole[1] * 32) & (hole[0] == kind), MASKED, s)
        return s

    def value(g, j):
        _, ref, first, count, part = plan[j]
        return values_of(ref, first, count, part)

    def finish(g, out):
        for h in range(HB):
            sl = pl.ds(pl.multiple_of((g * HB + h) * 128, 128), 128)
            gated = out[h * t : (h + 1) * t] * g_ref[g * HB + h, :, 0:1]
            out_ref[:, sl] = add_ref[:, sl] + gated

    attend_groups(qa_ref.shape[0] // HB, len(plan), coef, score, value, finish, nothing, refs)


TILES = 4


def selected_kernel(coef, chunk, index, qa_ref, qb_ref, g_ref, add_ref, *refs):
    gots, out_ref, buf, sem = refs[:4], refs[4], refs[5], refs[6]
    heads = qa_ref.shape[0]
    t = qa_ref.shape[1] // TILES
    rows = heads * t
    per = buf.shape[0] // TILES

    def fetch(n, carry):
        for k in range(4):
            @pl.when(chunk[n] == k)
            def _():
                pltpu.make_async_copy(gots[k].at[index[n]], buf.at[n], sem.at[n]).start()

        return carry

    lax.fori_loop(0, buf.shape[0], fetch, 0)

    def ready(g):
        def wait(j, carry):
            n = g * per + j
            pltpu.make_async_copy(gots[0].at[0], buf.at[n], sem.at[n]).wait()
            return carry

        lax.fori_loop(0, per, wait, 0)

    def tile(g):
        return pl.ds(pl.multiple_of(g * t, t), t)

    def score(g, j):
        q = (qa_ref, qb_ref)[j][:, tile(g), :].reshape(rows, 256)
        return nt_dot(q, part_of(buf, g * per, per, j))

    def value(g, j):
        return values_of(buf, g * per, per, j)

    def finish(g, out):
        for h in range(heads):
            hs = slice(128 * h, 128 * h + 128)
            gated = out[h * t : (h + 1) * t] * g_ref[h, tile(g), 1:2]
            out_ref[tile(g), hs] = (add_ref[tile(g), hs] + gated).astype(BF)

    attend_groups(TILES, 2, coef, score, value, finish, ready, refs[7:])


def cost(rows, keys):
    return pl.CostEstimate(
        flops=2 * rows * keys * 512, bytes_accessed=6 << 20, transcendentals=rows * keys
    )


def by_heads(kernel, scalars, args, moved, keys, dtype, scratch):
    heads, t, _ = args[0].shape
    whole = lambda a: pl.BlockSpec(a.shape, lambda i, *_, n=a.ndim: (0,) * n)
    return pl.pallas_call(
        kernel,
        grid_spec=pltpu.PrefetchScalarGridSpec(
            num_scalar_prefetch=len(scalars),
            grid=(1,),
            in_specs=[whole(a) for a in args] + [pl.BlockSpec(memory_space=pl.ANY) for _ in moved],
            out_specs=pl.BlockSpec((t, heads * 128), lambda i, *_: (0, 0)),
            scratch_shapes=scratch,
        ),
        out_shape=jax.ShapeDtypeStruct((t, heads * 128), dtype),
        cost_estimate=cost(heads * t, keys),
    )(*scalars, *args, *moved)


def swap(x):
    return lax.ppermute(x, "c", [(0, 1), (1, 0)])


def shards(
    queries,
    cache_keys,
    cache_values,
    incoming_keys,
    new_values,
    comp_key_weight,
    comp_value_weight,
    select_blocks,
    gate_weight,
):
    heads, key_width, _ = gate_weight.shape
    coef = key_width ** (-0.5) * math.log2(math.e)
    z, y, c = lax.axis_index("z"), lax.axis_index("y"), lax.axis_index("c")
    info = jnp.stack([c, lax.axis_index("kv")]).astype(jnp.int32)

    cache = pack(cache_keys, cache_values)
    own = pack(incoming_keys, new_values)
    near = jnp.concatenate([cache, own], axis=0)
    near_other = swap(near)
    other, mate = near_other[:16], near_other[16:]

    w_both, w_half = weight_pack(info, comp_key_weight.T, comp_value_weight)
    sides = [(2 * k, 2 * ((k + 1) % 4)) for k in range(4)]
    sides += [(2 * k + 1, 2 * ((k - 1) % 4) + 1) for k in range(4)]
    w1_mine = lax.ppermute(w_both, ("kv", "c"), sides)
    w2_mine = lax.ppermute(w_half, "kv", [(k, (k + 2) % 4) for k in range(4)])
    w1_other = swap(w1_mine)
    w2_other = swap(w2_mine)

    chosen = select_blocks.reshape(-1)
    shard, local = chosen >> 4, chosen & 15
    zs, ys, cs = shard >> 3, (shard >> 1) & 3, shard & 1
    n = chosen.shape[0]
    before = jnp.arange(n)[None, :] < jnp.arange(n)[:, None]
    order = jnp.sum(((shard[:, None] == shard[None, :]) & before).astype(jnp.int32), axis=1)
    delta = (z - zs) & 7
    up = (delta >= 1) & (delta <= 3)
    down = delta >= 5
    relay_core = jnp.where(up, 0, jnp.where(down, 1, cs))
    source = jnp.where(
        up,
        2 * delta - 1 + cs,
        jnp.where(down, 2 * (8 - delta) - 1 + (1 - cs), jnp.where(delta == 4, 7, 0)),
    )
    relay, slot = ys * 2 + relay_core, source * 2 + order
    flat = relay * 16 + slot
    request = jnp.sum(
        jnp.where(flat[None, :] == jnp.arange(128, dtype=jnp.int32)[:, None], local[None, :], 0),
        axis=1,
    ).reshape(Y * C, 16)
    rq = lax.all_to_all(request, ("y", "c"), split_axis=0, concat_axis=0, tiled=True)
    rq = jnp.clip(rq, 0, 15)
    chunk = jnp.zeros_like(slot)
    index = relay * 2 + slot
    for k, (low, high) in enumerate(((2, 6), (6, 10), (10, 16))):
        inside = slot >= low
        chunk = jnp.where(inside, k + 1, chunk)
        index = jnp.where(inside, relay * (high - low) + slot - low, index)

    chip = z * Y + y
    tail = jnp.where(c == 1, cache[8:16], other[8:16])
    last = chip == Z * Y - 1
    before1 = jnp.where(c == 0, tail[4:8], jnp.concatenate([tail[6:8], tail[4:6]]))
    ship = jnp.where(last, before1, jnp.concatenate([own, mate]))
    ship = jnp.concatenate([ship, other[15:16]])
    chips = Z * Y
    pairs = [(2 * q, 2 * ((q + 1) % chips)) for q in range(chips)]
    pairs += [(2 * q + 1, 2 * (q + 2) + 1) for q in range(chips - 2)]
    pairs += [(2 * (chips - 1) + 1, 3)]
    got = lax.ppermute(ship, ("z", "y", "c"), pairs)
    far = jnp.concatenate([tail[2:4], tail[0:2]])
    far = lax.ppermute(far, ("z", "y", "c"), [(2 * (chips - 1) + 1, 1)])
    wm = jnp.where((chip == 0) & (c == 1), far, got[:4])
    edge_block = jnp.where(c == 1, other[15], got[4])
    edge_v = edge_block[48:64]
    edge_k = jnp.concatenate([edge_block[112:128], edge_block[144:160, 64:128]], axis=1)

    ring = [(2 * k, 2 * ((k + 1) % Z)) for k in range(Z)]
    ring += [(2 * k + 1, 2 * ((k - 1) % Z) + 1) for k in range(Z)]
    pair = jnp.concatenate([cache, other], axis=0)
    steps = [pair]
    for k in range(1, 5):
        x = steps[-1] if k < 4 else steps[-1][:16]
        steps.append(lax.ppermute(x, ("z", "c"), ring))
    _, r1, r2, r3, r4 = steps

    def exchange(srcs, plan, first):
        sent = gather_blocks(srcs, plan, first, rq)
        return lax.all_to_all(sent, ("y", "c"), split_axis=0, concat_axis=0, tiled=True)

    twice = ((0, 0), (0, 0), (0, 16), (0, 16))
    gots = (
        exchange((cache,), twice[:2], 0),
        exchange((r1,), twice, 2),
        exchange((r2,), twice, 6),
        exchange((r3, r4), twice + ((1, 0), (1, 0)), 10),
    )

    g = jnp.pad(gate_weight.transpose(0, 2, 1), ((0, 0), (0, 5), (0, 256 - key_width)))
    qa, qb, g = query_layout(queries, g)
    t = queries.shape[0]
    wt = swap(wm)
    acc = by_heads(
        functools.partial(window_kernel, coef), (info,),
        (qa, qb, g, wm, wt, jnp.concatenate([own, mate])), (), 768, F32,
        [pltpu.VMEM((2, t, 384), F32)] + score_scratch(HB * t, 768),
    )

    xk = cache_keys.reshape(-1, 16 * key_width)
    xv = cache_values.reshape(-1, 16 * cache_values.shape[1])
    comp = compress(
        info, xk, xv, edge_k.reshape(1, -1), edge_v.reshape(1, -1),
        w_both, w1_mine, w2_mine, w1_other, w2_other,
    )
    column = [comp]
    for k in range(1, 4):
        column.append(lax.ppermute(comp, "y", [(i, (i + k) % Y) for i in range(Y)]))
    column = jnp.concatenate(column)
    plane = jnp.concatenate([column, swap(column)])
    by_two = [(2 * k, 2 * ((k + 2) % Z)) for k in range(Z)]
    by_two += [(2 * k + 1, 2 * ((k - 2) % Z) + 1) for k in range(Z)]
    one = lax.ppermute(plane, ("z", "c"), ring)
    two = lax.ppermute(plane, ("z", "c"), by_two)
    three = lax.ppermute(one, ("z", "c"), by_two)
    four = lax.ppermute(two[:4], ("z", "c"), by_two)
    mine = jnp.concatenate([one, two, three, four], axis=0)
    others = swap(mine)
    carrier = jnp.where(z <= 4, 0, 1)
    hole = jnp.stack(
        [
            jnp.where(z == 0, 0, jnp.where(carrier == c, 1, 2)),
            jnp.where(
                z == 0,
                y + 4 * c,
                y + 4 * carrier + 8 * (jnp.where(z <= 4, z, 8 - z) - 1),
            ),
        ]
    ).astype(jnp.int32)
    acc = by_heads(
        functools.partial(compressed_kernel, coef), (hole,),
        (qa, qb, g, plane, mine, others, acc), (), 4096, F32,
        score_scratch(HB * t, 4096),
    )
    return by_heads(
        functools.partial(selected_kernel, coef), (chunk, index),
        (qa, qb, g, acc), gots, 1024, BF,
        [pltpu.VMEM((n, ROWS, 128), BF), pltpu.SemaphoreType.DMA((n,))]
        + score_scratch(heads * t // TILES, 1024),
    )


def solution(mesh):
    wide = Mesh(mesh.devices.reshape(4, Z, Y, C), ("kv", "z", "y", "c"))
    seq = ("z", "y", "c")
    placed = (
        P(seq, "kv"),
        P(seq, "kv"),
        P(seq, "kv"),
        P(seq, "kv"),
        P(seq, "kv"),
        P("kv", None),
        P("kv", None),
        P(seq, "kv", None),
        P("kv", None, None),
    )
    return jax.shard_map(
        shards, mesh=wide, in_specs=placed, out_specs=P(seq, "kv"), check_vma=False
    )
```

```python
import functools
import math

import jax
import jax.numpy as jnp
from jax import lax
from jax.experimental import pallas as pl
from jax.experimental.pallas import tpu as pltpu
from jax.sharding import Mesh, PartitionSpec as P


BLOCK = 64
ROWS = 160
WINDOW = 512
MASKED = -1e30
BF = jnp.bfloat16
F32 = jnp.float32
Z, Y, C = 8, 4, 2


def limit(mib):
    return pltpu.CompilerParams(vmem_limit_bytes=mib << 20)


def pack(keys, values):
    k = keys.reshape(-1, BLOCK, keys.shape[1])
    v = values.reshape(-1, BLOCK, values.shape[1])
    high = jnp.concatenate([k[:, :32, 128:], k[:, 32:, 128:]], axis=2)
    return jnp.concatenate([v, k[:, :, :128], high], axis=1)


def nt_dot(a, b):
    return lax.dot_general(a, b, (((1,), (1,)), ((), ())), preferred_element_type=F32)


def stage(n, coef, score, value, ahead, now, finish):
    peak = acc = None
    at = 0
    for j in range(n):
        v = value(0 if now is None else now[0], j)
        w = v.shape[0]
        if ahead is not None:
            g, s_ref, m_ref = ahead
            s = score(g, j)
            s_ref[:, at : at + w] = s
            for k in range(0, w, 128):
                piece = s[:, k : k + 128]
                peak = piece if peak is None else jnp.maximum(peak, piece)
        if now is not None:
            g, s_ref, m_ref = now
            top = m_ref[...]
            p = [
                jnp.exp2(s_ref[:, k : k + 128] * coef - top).astype(BF)
                for k in range(at, at + w, 128)
            ]
            both = jnp.concatenate([v, jnp.ones_like(v)], axis=1)
            part = jnp.dot(jnp.concatenate(p, axis=1), both, preferred_element_type=F32)
            acc = part if acc is None else acc + part
        at += w
    if ahead is not None:
        m_ref = ahead[2]
        peak = jnp.max(peak, axis=1, keepdims=True) * coef
        m_ref[...] = jnp.broadcast_to(peak, m_ref.shape)
    if now is not None:
        finish(now[0], acc[:, :128] / acc[:, 128:])


def attend_groups(groups, n, coef, score, value, finish, ready, refs):
    sa, sb, ma, mb = refs
    ready(0)
    stage(n, coef, score, value, (0, sa, ma), None, finish)

    def body(i, carry):
        ready(2 * i + 1)
        stage(n, coef, score, value, (2 * i + 1, sb, mb), (2 * i, sa, ma), finish)

        @pl.when(2 * i + 2 < groups)
        def _():
            ready(2 * i + 2)
            stage(n, coef, score, value, (2 * i + 2, sa, ma), (2 * i + 1, sb, mb), finish)

        @pl.when(2 * i + 2 >= groups)
        def _():
            stage(n, coef, score, value, None, (2 * i + 1, sb, mb), finish)

        return carry

    lax.fori_loop(0, groups // 2, body, 0)


def score_scratch(rows, keys):
    return [pltpu.VMEM((rows, keys), F32)] * 2 + [pltpu.VMEM((rows, 128), F32)] * 2


def query_kernel(q_ref, g_ref, qa_ref, qb_ref, gate_ref):
    for h in range(qa_ref.shape[0]):
        x = q_ref[:, 192 * h : 192 * h + 192]
        zero = jnp.zeros((x.shape[0], 64), BF)
        qa = jnp.concatenate([x, zero], axis=1)
        qa_ref[h] = qa
        qb_ref[h] = jnp.concatenate([x[:, :128], zero, x[:, 128:]], axis=1)
        gate_ref[h] = jax.nn.sigmoid(nt_dot(qa, g_ref[h]))


def query_layout(queries, g):
    heads, t = g.shape[0], queries.shape[0]
    shape = jax.ShapeDtypeStruct((heads, t, 256), BF)
    return pl.pallas_call(
        query_kernel,
        out_shape=(shape, shape, jax.ShapeDtypeStruct((heads, t, 8), F32)),
        cost_estimate=pl.CostEstimate(flops=0, bytes_accessed=4 << 20, transcendentals=0),
        name="query_layout",
    )(queries, g)


def gather_kernel(plan, first, rq, *refs):
    srcs, (out_ref, buf, sem, out_sem) = refs[:-4], refs[-4:]
    width = len(plan)
    inward, outward = [], []
    for dest in range(Y * C):
        for s, (src, base) in enumerate(plan):
            i = dest * width + s
            copy = pltpu.make_async_copy(
                srcs[src].at[base + rq[dest, first + s]], buf.at[i], sem.at[i]
            )
            copy.start()
            inward.append(copy)
    for dest in range(Y * C):
        for copy in inward[dest * width : (dest + 1) * width]:
            copy.wait()
        span = pl.ds(dest * width, width)
        copy = pltpu.make_async_copy(buf.at[span], out_ref.at[span], out_sem.at[dest])
        copy.start()
        outward.append(copy)
    for copy in outward:
        copy.wait()


def gather_blocks(srcs, plan, first, rq):
    count = Y * C * len(plan)
    return pl.pallas_call(
        functools.partial(gather_kernel, plan, first),
        grid_spec=pltpu.PrefetchScalarGridSpec(
            num_scalar_prefetch=1,
            grid=(1,),
            in_specs=[pl.BlockSpec(memory_space=pl.ANY)] * len(srcs),
            out_specs=pl.BlockSpec(memory_space=pltpu.HBM),
            scratch_shapes=[
                pltpu.VMEM((count, ROWS, 128), BF),
                pltpu.SemaphoreType.DMA((count,)),
                pltpu.SemaphoreType.DMA((Y * C,)),
            ],
        ),
        out_shape=jax.ShapeDtypeStruct((count, ROWS, 128), BF),
        cost_estimate=pl.CostEstimate(
            flops=0, bytes_accessed=count * ROWS * 128 * 4, transcendentals=0
        ),
        compiler_params=limit(6),
        name="gather_blocks",
    )(rq, *srcs)


def weight_kernel(info, k_ref, v_ref, both_ref, half_ref):
    c = info[0]
    for h in range(2):
        for j in range(6):
            x = k_ref[:, 768 * h + 128 * j : 768 * h + 128 * j + 128]
            both_ref[h, 192 * j : 192 * j + 192, :] = x
        both_ref[h, 1152:1664, :] = v_ref[512 * h : 512 * h + 512, :]
    half_ref[...] = both_ref[c]


def weight_pack(info, wk, wv):
    whole = lambda a: pl.BlockSpec(a.shape, lambda i, c: (0, 0))
    return pl.pallas_call(
        weight_kernel,
        grid_spec=pltpu.PrefetchScalarGridSpec(
            num_scalar_prefetch=1,
            grid=(1,),
            in_specs=[whole(wk), whole(wv)],
            out_specs=(
                pl.BlockSpec((2, 1664, 128), lambda i, c: (0, 0, 0)),
                pl.BlockSpec((1664, 128), lambda i, c: (0, 0)),
            ),
        ),
        out_shape=(
            jax.ShapeDtypeStruct((2, 1664, 128), BF),
            jax.ShapeDtypeStruct((1664, 128), BF),
        ),
        cost_estimate=pl.CostEstimate(flops=0, bytes_accessed=3 << 20, transcendentals=0),
        name="weight_pack",
    )(info, wk, wv)


def compress_kernel(
    info, xk_ref, xv_ref, ek_ref, ev_ref, own_ref, m1_ref, m2_ref, o1_ref, o2_ref, out_ref
):
    c, x = info[0], info[1]
    row = lax.broadcasted_iota(jnp.int32, (64, 1), 0)

    def taken(ref, edge, start, width, first):
        span = pl.ds(start, width)
        a = ref[:, span].astype(F32)
        lead = jnp.where(row == 0, edge[:, span].astype(F32), jnp.roll(a, 1, axis=0))
        return jnp.where(first, lead, a).astype(BF)

    step = 1 - 2 * c
    near, far, across = (x - step) & 3, (x + step) & 3, (x + 2) & 3
    pieces = [(own_ref.at[h], x, h) for h in range(2)]
    pieces += [(m1_ref.at[h], near, h) for h in range(2)]
    pieces += [(o1_ref.at[h], far, h) for h in range(2)]
    pieces += [(m2_ref, across, c), (o2_ref, across, 1 - c)]
    keys = jnp.zeros((64, 192), F32)
    values = jnp.zeros((64, 128), F32)
    for ref, i, h in pieces:
        at = 8 * (i & 1) + 4 * h
        a = taken(xk_ref, ek_ref, pl.multiple_of(at * 192, 256), 768, i < 2)
        for j in range(3):
            w = jnp.concatenate(
                [ref[384 * j : 384 * j + 192, :], ref[384 * j + 192 : 384 * j + 384, :]], axis=1
            )
            keys = keys + nt_dot(a[:, 256 * j : 256 * j + 256], w)
        a = taken(xv_ref, ev_ref, pl.multiple_of(at * 128, 512), 512, i < 2)
        values = values + jnp.dot(a, ref[1152:1664, :], preferred_element_type=F32)
    keys = keys.astype(BF)
    out_ref[0, 0:64, :] = values.astype(BF)
    out_ref[0, 64:128, :] = keys[:, :128]
    out_ref[0, 128:160, :] = jnp.concatenate([keys[:32, 128:], keys[32:, 128:]], axis=1)


def compress(info, *args):
    full = lambda a: pl.BlockSpec(a.shape, lambda i, c, n=a.ndim: (0,) * n)
    return pl.pallas_call(
        compress_kernel,
        grid_spec=pltpu.PrefetchScalarGridSpec(
            num_scalar_prefetch=1,
            grid=(1,),
            in_specs=[full(a) for a in args],
            out_specs=pl.BlockSpec((1, ROWS, 128), lambda i, c: (0, 0, 0)),
        ),
        out_shape=jax.ShapeDtypeStruct((1, ROWS, 128), BF),
        cost_estimate=pl.CostEstimate(
            flops=2 * 64 * (6144 * 192 + 4096 * 128), bytes_accessed=4 << 20, transcendentals=0
        ),
        name="compress",
    )(info, *args)


HB = 4


def part_of(ref, first, count, part):
    n = count * 32
    blocks = pl.ds(first, count)
    low = ref[blocks, 64 + 32 * part : 96 + 32 * part, :].reshape(n, 128)
    high = ref[blocks, 128:160, :].reshape(n, 128)
    return jnp.concatenate([low, high], axis=1)


def values_of(ref, first, count, part):
    return ref[pl.ds(first, count), 32 * part : 32 * part + 32, :].reshape(count * 32, 128)


def nothing(g):
    pass


def window_kernel(coef, core, qa_ref, qb_ref, g_ref, wm_ref, wt_ref, own_ref, out_ref, bias, *refs):
    c = core[0]
    t = qa_ref.shape[1]
    rows = HB * t
    plan = ((wm_ref, -256 - 256 * c, c), (wt_ref, -512 + 256 * c, 1 - c), (own_ref, 0, c))
    at = lax.broadcasted_iota(jnp.int32, (t, 1), 0) + c * t
    for part in range(2):
        for k, (ref, base, ring) in enumerate(plan):
            i = lax.broadcasted_iota(jnp.int32, (1, 128), 1)
            which = lax.shift_right_logical(i, 6)
            which = which + ring - 2 * which * ring
            where = base + which * t + (lax.shift_right_logical(i, 5) & 1) * 64 + part * 32
            where = where + (i & 31)
            ok = (where <= at) & (where > at - WINDOW)
            bias[part, :, 128 * k : 128 * k + 128] = jnp.where(ok, 0.0, MASKED)

    def score(g, j):
        q = (qa_ref, qb_ref)[j][pl.ds(g * HB, HB)].reshape(rows, 256)
        k = jnp.concatenate([part_of(ref, 0, 4, j) for ref, _, _ in plan], axis=0)
        s = nt_dot(q, k).reshape(HB, t, 384) + bias[j][None]
        return s.reshape(rows, 384)

    def value(g, j):
        return jnp.concatenate([values_of(ref, 0, 4, j) for ref, _, _ in plan], axis=0)

    def finish(g, out):
        for h in range(HB):
            sl = pl.ds(pl.multiple_of((g * HB + h) * 128, 128), 128)
            out_ref[:, sl] = out[h * t : (h + 1) * t] * g_ref[g * HB + h, :, 2:3]

    attend_groups(qa_ref.shape[0] // HB, 2, coef, score, value, finish, nothing, refs)


def compressed_kernel(
    coef, hole, qa_ref, qb_ref, g_ref, add_ref, *refs
):
    blocks, out_ref, refs = refs[:5], refs[5], refs[6:]
    t = qa_ref.shape[1]
    rows = HB * t
    plan = []
    for kind, ref in enumerate(blocks):
        for first in range(0, ref.shape[0], 16):
            for part in range(2):
                plan.append((kind, ref, first, min(16, ref.shape[0] - first), part))

    def score(g, j):
        kind, ref, first, count, part = plan[j]
        q = (qa_ref, qb_ref)[part][pl.ds(g * HB, HB)].reshape(rows, 256)
        s = nt_dot(q, part_of(ref, first, count, part))
        if part == 0:
            col = lax.broadcasted_iota(jnp.int32, (1, count * 32), 1) + first * 32
            s = jnp.where((col == hole[1] * 32) & (hole[0] == kind), MASKED, s)
        return s

    def value(g, j):
        _, ref, first, count, part = plan[j]
        return values_of(ref, first, count, part)

    def finish(g, out):
        for h in range(HB):
            sl = pl.ds(pl.multiple_of((g * HB + h) * 128, 128), 128)
            gated = out[h * t : (h + 1) * t] * g_ref[g * HB + h, :, 0:1]
            out_ref[:, sl] = add_ref[:, sl] + gated

    attend_groups(qa_ref.shape[0] // HB, len(plan), coef, score, value, finish, nothing, refs)


TILES = 4


def selected_kernel(coef, chunk, index, qa_ref, qb_ref, g_ref, add_ref, *refs):
    gots, out_ref, buf, sem = refs[:4], refs[4], refs[5], refs[6]
    heads = qa_ref.shape[0]
    t = qa_ref.shape[1] // TILES
    rows = heads * t
    per = buf.shape[0] // TILES

    def fetch(n, carry):
        for k in range(4):
            @pl.when(chunk[n] == k)
            def _():
                pltpu.make_async_copy(gots[k].at[index[n]], buf.at[n], sem.at[n]).start()

        return carry

    lax.fori_loop(0, buf.shape[0], fetch, 0)

    def ready(g):
        def wait(j, carry):
            n = g * per + j
            pltpu.make_async_copy(gots[0].at[0], buf.at[n], sem.at[n]).wait()
            return carry

        lax.fori_loop(0, per, wait, 0)

    def tile(g):
        return pl.ds(pl.multiple_of(g * t, t), t)

    def score(g, j):
        q = (qa_ref, qb_ref)[j][:, tile(g), :].reshape(rows, 256)
        return nt_dot(q, part_of(buf, g * per, per, j))

    def value(g, j):
        return values_of(buf, g * per, per, j)

    def finish(g, out):
        for h in range(heads):
            hs = slice(128 * h, 128 * h + 128)
            gated = out[h * t : (h + 1) * t] * g_ref[h, tile(g), 1:2]
            out_ref[tile(g), hs] = (add_ref[tile(g), hs] + gated).astype(BF)

    attend_groups(TILES, 2, coef, score, value, finish, ready, refs[7:])


def cost(rows, keys):
    return pl.CostEstimate(
        flops=2 * rows * keys * 512, bytes_accessed=6 << 20, transcendentals=rows * keys
    )


def by_heads(kernel, scalars, args, moved, keys, dtype, scratch):
    heads, t, _ = args[0].shape
    whole = lambda a: pl.BlockSpec(a.shape, lambda i, *_, n=a.ndim: (0,) * n)
    return pl.pallas_call(
        kernel,
        grid_spec=pltpu.PrefetchScalarGridSpec(
            num_scalar_prefetch=len(scalars),
            grid=(1,),
            in_specs=[whole(a) for a in args] + [pl.BlockSpec(memory_space=pl.ANY) for _ in moved],
            out_specs=pl.BlockSpec((t, heads * 128), lambda i, *_: (0, 0)),
            scratch_shapes=scratch,
        ),
        out_shape=jax.ShapeDtypeStruct((t, heads * 128), dtype),
        cost_estimate=cost(heads * t, keys),
    )(*scalars, *args, *moved)


def swap(x):
    return lax.ppermute(x, "c", [(0, 1), (1, 0)])


def shards(
    queries,
    cache_keys,
    cache_values,
    incoming_keys,
    new_values,
    comp_key_weight,
    comp_value_weight,
    select_blocks,
    gate_weight,
):
    heads, key_width, _ = gate_weight.shape
    coef = key_width ** (-0.5) * math.log2(math.e)
    z, y, c = lax.axis_index("z"), lax.axis_index("y"), lax.axis_index("c")
    info = jnp.stack([c, lax.axis_index("kv")]).astype(jnp.int32)

    cache = pack(cache_keys, cache_values)
    own = pack(incoming_keys, new_values)
    near = jnp.concatenate([cache, own], axis=0)
    near_other = swap(near)
    other, mate = near_other[:16], near_other[16:]

    w_both, w_half = weight_pack(info, comp_key_weight.T, comp_value_weight)
    sides = [(2 * k, 2 * ((k + 1) % 4)) for k in range(4)]
    sides += [(2 * k + 1, 2 * ((k - 1) % 4) + 1) for k in range(4)]
    w1_mine = lax.ppermute(w_both, ("kv", "c"), sides)
    w2_mine = lax.ppermute(w_half, "kv", [(k, (k + 2) % 4) for k in range(4)])
    w1_other = swap(w1_mine)
    w2_other = swap(w2_mine)

    chosen = select_blocks.reshape(-1)
    shard, local = chosen >> 4, chosen & 15
    zs, ys, cs = shard >> 3, (shard >> 1) & 3, shard & 1
    n = chosen.shape[0]
    before = jnp.arange(n)[None, :] < jnp.arange(n)[:, None]
    order = jnp.sum(((shard[:, None] == shard[None, :]) & before).astype(jnp.int32), axis=1)
    delta = (z - zs) & 7
    up = (delta >= 1) & (delta <= 3)
    down = delta >= 5
    relay_core = jnp.where(up, 0, jnp.where(down, 1, cs))
    source = jnp.where(
        up,
        2 * delta - 1 + cs,
        jnp.where(down, 2 * (8 - delta) - 1 + (1 - cs), jnp.where(delta == 4, 7, 0)),
    )
    relay, slot = ys * 2 + relay_core, source * 2 + order
    flat = relay * 16 + slot
    request = jnp.sum(
        jnp.where(flat[None, :] == jnp.arange(128, dtype=jnp.int32)[:, None], local[None, :], 0),
        axis=1,
    ).reshape(Y * C, 16)
    rq = lax.all_to_all(request, ("y", "c"), split_axis=0, concat_axis=0, tiled=True)
    rq = jnp.clip(rq, 0, 15)
    chunk = jnp.zeros_like(slot)
    index = relay * 2 + slot
    for k, (low, high) in enumerate(((2, 6), (6, 10), (10, 16))):
        inside = slot >= low
        chunk = jnp.where(inside, k + 1, chunk)
        index = jnp.where(inside, relay * (high - low) + slot - low, index)

    chip = z * Y + y
    tail = jnp.where(c == 1, cache[8:16], other[8:16])
    last = chip == Z * Y - 1
    before1 = jnp.where(c == 0, tail[4:8], jnp.concatenate([tail[6:8], tail[4:6]]))
    ship = jnp.where(last, before1, jnp.concatenate([own, mate]))
    ship = jnp.concatenate([ship, other[15:16]])
    chips = Z * Y
    pairs = [(2 * q, 2 * ((q + 1) % chips)) for q in range(chips)]
    pairs += [(2 * q + 1, 2 * (q + 2) + 1) for q in range(chips - 2)]
    pairs += [(2 * (chips - 1) + 1, 3)]
    got = lax.ppermute(ship, ("z", "y", "c"), pairs)
    far = jnp.concatenate([tail[2:4], tail[0:2]])
    far = lax.ppermute(far, ("z", "y", "c"), [(2 * (chips - 1) + 1, 1)])
    wm = jnp.where((chip == 0) & (c == 1), far, got[:4])
    edge_block = jnp.where(c == 1, other[15], got[4])
    edge_v = edge_block[48:64]
    edge_k = jnp.concatenate([edge_block[112:128], edge_block[144:160, 64:128]], axis=1)

    ring = [(2 * k, 2 * ((k + 1) % Z)) for k in range(Z)]
    ring += [(2 * k + 1, 2 * ((k - 1) % Z) + 1) for k in range(Z)]
    pair = jnp.concatenate([cache, other], axis=0)
    steps = [pair]
    for k in range(1, 5):
        x = steps[-1] if k < 4 else steps[-1][:16]
        steps.append(lax.ppermute(x, ("z", "c"), ring))
    _, r1, r2, r3, r4 = steps

    def exchange(srcs, plan, first):
        sent = gather_blocks(srcs, plan, first, rq)
        return lax.all_to_all(sent, ("y", "c"), split_axis=0, concat_axis=0, tiled=True)

    twice = ((0, 0), (0, 0), (0, 16), (0, 16))
    gots = (
        exchange((cache,), twice[:2], 0),
        exchange((r1,), twice, 2),
        exchange((r2,), twice, 6),
        exchange((r3, r4), twice + ((1, 0), (1, 0)), 10),
    )

    g = jnp.pad(gate_weight.transpose(0, 2, 1), ((0, 0), (0, 5), (0, 256 - key_width)))
    qa, qb, g = query_layout(queries, g)
    t = queries.shape[0]
    wt = swap(wm)
    acc = by_heads(
        functools.partial(window_kernel, coef), (info,),
        (qa, qb, g, wm, wt, jnp.concatenate([own, mate])), (), 768, F32,
        [pltpu.VMEM((2, t, 384), F32)] + score_scratch(HB * t, 768),
    )

    xk = cache_keys.reshape(-1, 16 * key_width)
    xv = cache_values.reshape(-1, 16 * cache_values.shape[1])
    comp = compress(
        info, xk, xv, edge_k.reshape(1, -1), edge_v.reshape(1, -1),
        w_both, w1_mine, w2_mine, w1_other, w2_other,
    )
    column = [comp]
    for k in range(1, 4):
        column.append(lax.ppermute(comp, "y", [(i, (i + k) % Y) for i in range(Y)]))
    column = lax.optimization_barrier(jnp.concatenate(column))
    plane = jnp.concatenate([column, swap(column)])
    by_two = [(2 * k, 2 * ((k + 2) % Z)) for k in range(Z)]
    by_two += [(2 * k + 1, 2 * ((k - 2) % Z) + 1) for k in range(Z)]
    one = lax.ppermute(plane, ("z", "c"), ring)
    two = lax.ppermute(plane, ("z", "c"), by_two)
    three = lax.ppermute(one, ("z", "c"), by_two)
    four = lax.ppermute(two[:4], ("z", "c"), by_two)
    near_mine = jnp.concatenate([one, two], axis=0)
    far_mine = jnp.concatenate([three, four], axis=0)
    near_other = swap(near_mine)
    far_other = swap(far_mine)
    away = jnp.where(z <= 4, z, 8 - z) - 1
    carrier = jnp.where(z <= 4, 0, 1)
    hole = jnp.stack(
        [
            jnp.where(z == 0, 0, jnp.where(carrier == c, 1, 3) + (away >= 2)),
            jnp.where(z == 0, y + 4 * c, y + 4 * carrier + 8 * (away & 1)),
        ]
    ).astype(jnp.int32)
    acc = by_heads(
        functools.partial(compressed_kernel, coef), (hole,),
        (qa, qb, g, acc, plane, near_mine, far_mine, near_other, far_other), (), 4096, F32,
        score_scratch(HB * t, 4096),
    )
    return by_heads(
        functools.partial(selected_kernel, coef), (chunk, index),
        (qa, qb, g, acc), gots, 1024, BF,
        [pltpu.VMEM((n, ROWS, 128), BF), pltpu.SemaphoreType.DMA((n,))]
        + score_scratch(heads * t // TILES, 1024),
    )


def solution(mesh):
    wide = Mesh(mesh.devices.reshape(4, Z, Y, C), ("kv", "z", "y", "c"))
    seq = ("z", "y", "c")
    placed = (
        P(seq, "kv"),
        P(seq, "kv"),
        P(seq, "kv"),
        P(seq, "kv"),
        P(seq, "kv"),
        P("kv", None),
        P("kv", None),
        P(seq, "kv", None),
        P("kv", None, None),
    )
    return jax.shard_map(
        shards, mesh=wide, in_specs=placed, out_specs=P(seq, "kv"), check_vma=False
    )
```

```python
import functools
import math

import jax
import jax.numpy as jnp
from jax import lax
from jax.experimental import pallas as pl
from jax.experimental.pallas import tpu as pltpu
from jax.sharding import Mesh, PartitionSpec as P


BLOCK = 64
ROWS = 160
WINDOW = 512
MASKED = -1e30
BF = jnp.bfloat16
F32 = jnp.float32
Z, Y, C = 8, 4, 2


def limit(mib):
    return pltpu.CompilerParams(vmem_limit_bytes=mib << 20)


def pack(keys, values):
    k = keys.reshape(-1, BLOCK, keys.shape[1])
    v = values.reshape(-1, BLOCK, values.shape[1])
    high = jnp.concatenate([k[:, :32, 128:], k[:, 32:, 128:]], axis=2)
    return jnp.concatenate([v, k[:, :, :128], high], axis=1)


def nt_dot(a, b):
    return lax.dot_general(a, b, (((1,), (1,)), ((), ())), preferred_element_type=F32)


def stage(n, coef, score, value, ahead, now, finish):
    peak = acc = None
    at = 0
    for j in range(n):
        v = value(0 if now is None else now[0], j)
        w = v.shape[0]
        if ahead is not None:
            g, s_ref, m_ref = ahead
            s = score(g, j)
            s_ref[:, at : at + w] = s
            for k in range(0, w, 128):
                piece = s[:, k : k + 128]
                peak = piece if peak is None else jnp.maximum(peak, piece)
        if now is not None:
            g, s_ref, m_ref = now
            top = m_ref[...]
            p = [
                jnp.exp2(s_ref[:, k : k + 128] * coef - top).astype(BF)
                for k in range(at, at + w, 128)
            ]
            both = jnp.concatenate([v, jnp.ones_like(v)], axis=1)
            part = jnp.dot(jnp.concatenate(p, axis=1), both, preferred_element_type=F32)
            acc = part if acc is None else acc + part
        at += w
    if ahead is not None:
        m_ref = ahead[2]
        peak = jnp.max(peak, axis=1, keepdims=True) * coef
        m_ref[...] = jnp.broadcast_to(peak, m_ref.shape)
    if now is not None:
        finish(now[0], acc[:, :128] / acc[:, 128:])


def attend_groups(groups, n, coef, score, value, finish, ready, refs):
    sa, sb, ma, mb = refs
    ready(0)
    stage(n, coef, score, value, (0, sa, ma), None, finish)

    def body(i, carry):
        ready(2 * i + 1)
        stage(n, coef, score, value, (2 * i + 1, sb, mb), (2 * i, sa, ma), finish)

        @pl.when(2 * i + 2 < groups)
        def _():
            ready(2 * i + 2)
            stage(n, coef, score, value, (2 * i + 2, sa, ma), (2 * i + 1, sb, mb), finish)

        @pl.when(2 * i + 2 >= groups)
        def _():
            stage(n, coef, score, value, None, (2 * i + 1, sb, mb), finish)

        return carry

    lax.fori_loop(0, groups // 2, body, 0)


def score_scratch(rows, keys):
    return [pltpu.VMEM((rows, keys), F32)] * 2 + [pltpu.VMEM((rows, 128), F32)] * 2


def query_kernel(q_ref, g_ref, qa_ref, qb_ref, gate_ref):
    heads = qa_ref.shape[0]
    gates = jnp.concatenate([g_ref[b] for b in range(3)], axis=0)
    for h in range(heads):
        x = q_ref[:, 192 * h : 192 * h + 192]
        zero = jnp.zeros((x.shape[0], 64), BF)
        qa = jnp.concatenate([x, zero], axis=1)
        qa_ref[h] = qa
        qb_ref[h] = jnp.concatenate([x[:, :128], zero, x[:, 128:]], axis=1)
        logits = nt_dot(x, gates)
        for b in range(3):
            at = b * heads + h
            gate_ref[h, :, b : b + 1] = jax.nn.sigmoid(logits[:, at : at + 1])


def query_layout(queries, g):
    heads, t = g.shape[1], queries.shape[0]
    shape = jax.ShapeDtypeStruct((heads, t, 256), BF)
    return pl.pallas_call(
        query_kernel,
        out_shape=(shape, shape, jax.ShapeDtypeStruct((heads, t, 8), F32)),
        cost_estimate=pl.CostEstimate(flops=0, bytes_accessed=4 << 20, transcendentals=0),
        name="query_layout",
    )(queries, g)


def gather_kernel(plan, first, rq, *refs):
    srcs, out_ref, sem = refs[:-2], refs[-2], refs[-1]
    width = len(plan)
    copies = []
    for dest in range(Y * C):
        for s, (src, base) in enumerate(plan):
            i = dest * width + s
            copy = pltpu.make_async_copy(
                srcs[src].at[base + rq[dest, first + s]], out_ref.at[i], sem.at[i]
            )
            copy.start()
            copies.append(copy)
    for copy in copies:
        copy.wait()


def gather_blocks(srcs, plan, first, rq, loaded=()):
    specs = [pl.BlockSpec(memory_space=pl.ANY)] * len(srcs)
    for k in loaded:
        specs[k] = pl.BlockSpec(srcs[k].shape, lambda i, rq: (0, 0, 0))
    count = Y * C * len(plan)
    return pl.pallas_call(
        functools.partial(gather_kernel, plan, first),
        grid_spec=pltpu.PrefetchScalarGridSpec(
            num_scalar_prefetch=1,
            grid=(1,),
            in_specs=specs,
            out_specs=pl.BlockSpec(memory_space=pltpu.HBM),
            scratch_shapes=[pltpu.SemaphoreType.DMA((count,))],
        ),
        out_shape=jax.ShapeDtypeStruct((count, ROWS, 128), BF),
        cost_estimate=pl.CostEstimate(
            flops=0, bytes_accessed=count * ROWS * 128 * 4, transcendentals=0
        ),
        compiler_params=limit(4),
        name="gather_blocks",
    )(rq, *srcs)


def weight_kernel(info, k_ref, v_ref, both_ref, half_ref):
    c = info[0]
    for h in range(2):
        for j in range(6):
            x = k_ref[:, 768 * h + 128 * j : 768 * h + 128 * j + 128]
            both_ref[h, 192 * j : 192 * j + 192, :] = x
        both_ref[h, 1152:1664, :] = v_ref[512 * h : 512 * h + 512, :]
    half_ref[...] = both_ref[c]


def weight_pack(info, wk, wv):
    whole = lambda a: pl.BlockSpec(a.shape, lambda i, c: (0, 0))
    return pl.pallas_call(
        weight_kernel,
        grid_spec=pltpu.PrefetchScalarGridSpec(
            num_scalar_prefetch=1,
            grid=(1,),
            in_specs=[whole(wk), whole(wv)],
            out_specs=(
                pl.BlockSpec((2, 1664, 128), lambda i, c: (0, 0, 0)),
                pl.BlockSpec((1664, 128), lambda i, c: (0, 0)),
            ),
        ),
        out_shape=(
            jax.ShapeDtypeStruct((2, 1664, 128), BF),
            jax.ShapeDtypeStruct((1664, 128), BF),
        ),
        cost_estimate=pl.CostEstimate(flops=0, bytes_accessed=3 << 20, transcendentals=0),
        name="weight_pack",
    )(info, wk, wv)


def compress_kernel(
    info, xk_ref, xv_ref, ea_ref, eb_ref, own_ref, m1_ref, m2_ref, o1_ref, o2_ref, out_ref,
    ek_ref, ev_ref,
):
    c, x = info[0], info[1]
    edge = jnp.where(c == 1, ea_ref[0].astype(F32), eb_ref[0].astype(F32))
    ev_ref[...] = edge[48:64]
    ek_ref[...] = jnp.concatenate([edge[112:128], edge[144:160, 64:128]], axis=1)
    row = lax.broadcasted_iota(jnp.int32, (64, 1), 0)

    def taken(ref, edge, at, width, first):
        a = ref[:, pl.ds(pl.multiple_of(at * width, 256), 4 * width)].astype(F32)
        before = jnp.concatenate([edge[pl.ds(at + k, 1), :] for k in range(4)], axis=1)
        lead = jnp.where(row == 0, before, jnp.roll(a, 1, axis=0))
        return jnp.where(first, lead, a).astype(BF)

    step = 1 - 2 * c
    near, far, across = (x - step) & 3, (x + step) & 3, (x + 2) & 3
    pieces = [(own_ref.at[h], x, h) for h in range(2)]
    pieces += [(m1_ref.at[h], near, h) for h in range(2)]
    pieces += [(o1_ref.at[h], far, h) for h in range(2)]
    pieces += [(m2_ref, across, c), (o2_ref, across, 1 - c)]
    keys = jnp.zeros((64, 192), F32)
    values = jnp.zeros((64, 128), F32)
    for ref, i, h in pieces:
        at = 8 * (i & 1) + 4 * h
        a = taken(xk_ref, ek_ref, at, 192, i < 2)
        for j in range(3):
            w = jnp.concatenate(
                [ref[384 * j : 384 * j + 192, :], ref[384 * j + 192 : 384 * j + 384, :]], axis=1
            )
            keys = keys + nt_dot(a[:, 256 * j : 256 * j + 256], w)
        a = taken(xv_ref, ev_ref, at, 128, i < 2)
        values = values + jnp.dot(a, ref[1152:1664, :], preferred_element_type=F32)
    keys = keys.astype(BF)
    out_ref[0, 0:64, :] = values.astype(BF)
    out_ref[0, 64:128, :] = keys[:, :128]
    out_ref[0, 128:160, :] = jnp.concatenate([keys[:32, 128:], keys[32:, 128:]], axis=1)


def compress(info, *args):
    full = lambda a: pl.BlockSpec(a.shape, lambda i, c, n=a.ndim: (0,) * n)
    return pl.pallas_call(
        compress_kernel,
        grid_spec=pltpu.PrefetchScalarGridSpec(
            num_scalar_prefetch=1,
            grid=(1,),
            in_specs=[full(a) for a in args[:2]]
            + [pl.BlockSpec((1, ROWS, 128), lambda i, c, k=k: (k, 0, 0)) for k in (15, 4)]
            + [full(a) for a in args[4:]],
            out_specs=pl.BlockSpec((1, ROWS, 128), lambda i, c: (0, 0, 0)),
            scratch_shapes=[pltpu.VMEM((16, 192), F32), pltpu.VMEM((16, 128), F32)],
        ),
        out_shape=jax.ShapeDtypeStruct((1, ROWS, 128), BF),
        cost_estimate=pl.CostEstimate(
            flops=2 * 64 * (6144 * 192 + 4096 * 128), bytes_accessed=4 << 20, transcendentals=0
        ),
        name="compress",
    )(info, *args)


HB = 4


def part_of(ref, first, count, part):
    n = count * 32
    blocks = pl.ds(first, count)
    low = ref[blocks, 64 + 32 * part : 96 + 32 * part, :].reshape(n, 128)
    high = ref[blocks, 128:160, :].reshape(n, 128)
    return jnp.concatenate([low, high], axis=1)


def values_of(ref, first, count, part):
    return ref[pl.ds(first, count), 32 * part : 32 * part + 32, :].reshape(count * 32, 128)


def nothing(g):
    pass


def window_kernel(
    coef, info, qa_ref, qb_ref, g_ref, got_ref, turned_ref, far_ref, own_ref, out_ref,
    wm_ref, wt_ref, bias, *refs
):
    c = info[0]
    first = info[2] == 0
    wm_ref[...] = jnp.where(first & (c == 1), far_ref[...], got_ref[0:4])
    wt_ref[...] = jnp.where(first & (c == 0), far_ref[...], turned_ref[0:4])
    t = qa_ref.shape[1]
    rows = HB * t
    plan = ((wm_ref, -256 - 256 * c, c), (wt_ref, -512 + 256 * c, 1 - c), (own_ref, 0, c))
    at = lax.broadcasted_iota(jnp.int32, (t, 1), 0) + c * t
    for part in range(2):
        for k, (ref, base, ring) in enumerate(plan):
            i = lax.broadcasted_iota(jnp.int32, (1, 128), 1)
            which = lax.shift_right_logical(i, 6)
            which = which + ring - 2 * which * ring
            where = base + which * t + (lax.shift_right_logical(i, 5) & 1) * 64 + part * 32
            where = where + (i & 31)
            ok = (where <= at) & (where > at - WINDOW)
            bias[part, :, 128 * k : 128 * k + 128] = jnp.where(ok, 0.0, MASKED)

    def score(g, j):
        q = (qa_ref, qb_ref)[j][pl.ds(g * HB, HB)].reshape(rows, 256)
        k = jnp.concatenate([part_of(ref, 0, 4, j) for ref, _, _ in plan], axis=0)
        s = nt_dot(q, k).reshape(HB, t, 384) + bias[j][None]
        return s.reshape(rows, 384)

    def value(g, j):
        return jnp.concatenate([values_of(ref, 0, 4, j) for ref, _, _ in plan], axis=0)

    def finish(g, out):
        for h in range(HB):
            sl = pl.ds(pl.multiple_of((g * HB + h) * 128, 128), 128)
            out_ref[:, sl] = out[h * t : (h + 1) * t] * g_ref[g * HB + h, :, 2:3]

    attend_groups(qa_ref.shape[0] // HB, 2, coef, score, value, finish, nothing, refs)


def compressed_kernel(
    coef, hole, qa_ref, qb_ref, g_ref, add_ref, *refs
):
    blocks, out_ref, refs = refs[:9], refs[9], refs[10:]
    t = qa_ref.shape[1]
    rows = HB * t
    plan = [
        (kinds, part) for kinds in ((0, 4, 8), (1, 2), (3, 5), (6, 7)) for part in range(2)
    ]

    def score(g, j):
        kinds, part = plan[j]
        q = (qa_ref, qb_ref)[part][pl.ds(g * HB, HB)].reshape(rows, 256)
        keys = [part_of(blocks[k], 0, blocks[k].shape[0], part) for k in kinds]
        s = nt_dot(q, jnp.concatenate(keys, axis=0))
        if part == 0:
            at = jnp.int32(-1)
            start = 0
            for k in kinds:
                at = jnp.where(hole[0] == k, start + hole[1] * 32, at)
                start += blocks[k].shape[0] * 32
            col = lax.broadcasted_iota(jnp.int32, (1, start), 1)
            s = jnp.where(col == at, MASKED, s)
        return s

    def value(g, j):
        kinds, part = plan[j]
        v = [values_of(blocks[k], 0, blocks[k].shape[0], part) for k in kinds]
        return jnp.concatenate(v, axis=0)

    def finish(g, out):
        for h in range(HB):
            sl = pl.ds(pl.multiple_of((g * HB + h) * 128, 128), 128)
            gated = out[h * t : (h + 1) * t] * g_ref[g * HB + h, :, 0:1]
            out_ref[:, sl] = add_ref[:, sl] + gated

    attend_groups(qa_ref.shape[0] // HB, len(plan), coef, score, value, finish, nothing, refs)


TILES = 4


def selected_kernel(coef, chunk, index, qa_ref, qb_ref, g_ref, add_ref, *refs):
    gots, out_ref, buf, sem = refs[:3], refs[3], refs[4], refs[5]
    heads = qa_ref.shape[0]
    t = qa_ref.shape[1] // TILES
    rows = heads * t
    per = buf.shape[0] // TILES

    def fetch(n, carry):
        for k in range(3):
            @pl.when(chunk[n] == k)
            def _():
                pltpu.make_async_copy(gots[k].at[index[n]], buf.at[n], sem.at[n]).start()

        return carry

    lax.fori_loop(0, buf.shape[0], fetch, 0)

    def ready(g):
        def wait(j, carry):
            n = g * per + j
            pltpu.make_async_copy(gots[0].at[0], buf.at[n], sem.at[n]).wait()
            return carry

        lax.fori_loop(0, per, wait, 0)

    def tile(g):
        return pl.ds(pl.multiple_of(g * t, t), t)

    def score(g, j):
        q = (qa_ref, qb_ref)[j][:, tile(g), :].reshape(rows, 256)
        return nt_dot(q, part_of(buf, g * per, per, j))

    def value(g, j):
        return values_of(buf, g * per, per, j)

    def finish(g, out):
        for h in range(heads):
            hs = slice(128 * h, 128 * h + 128)
            gated = out[h * t : (h + 1) * t] * g_ref[h, tile(g), 1:2]
            out_ref[tile(g), hs] = (add_ref[tile(g), hs] + gated).astype(BF)

    attend_groups(TILES, 2, coef, score, value, finish, ready, refs[6:])


def cost(rows, keys):
    return pl.CostEstimate(
        flops=2 * rows * keys * 512, bytes_accessed=6 << 20, transcendentals=rows * keys
    )


def by_heads(kernel, scalars, args, moved, keys, dtype, scratch):
    heads, t, _ = args[0].shape
    whole = lambda a: pl.BlockSpec(a.shape, lambda i, *_, n=a.ndim: (0,) * n)
    return pl.pallas_call(
        kernel,
        grid_spec=pltpu.PrefetchScalarGridSpec(
            num_scalar_prefetch=len(scalars),
            grid=(1,),
            in_specs=[whole(a) for a in args] + [pl.BlockSpec(memory_space=pl.ANY) for _ in moved],
            out_specs=pl.BlockSpec((t, heads * 128), lambda i, *_: (0, 0)),
            scratch_shapes=scratch,
        ),
        out_shape=jax.ShapeDtypeStruct((t, heads * 128), dtype),
        cost_estimate=cost(heads * t, keys),
    )(*scalars, *args, *moved)


def swap(x):
    return lax.ppermute(x, "c", [(0, 1), (1, 0)])


def shards(
    queries,
    cache_keys,
    cache_values,
    incoming_keys,
    new_values,
    comp_key_weight,
    comp_value_weight,
    select_blocks,
    gate_weight,
):
    heads, key_width, _ = gate_weight.shape
    coef = key_width ** (-0.5) * math.log2(math.e)
    z, y, c = lax.axis_index("z"), lax.axis_index("y"), lax.axis_index("c")
    chip = z * Y + y
    info = jnp.stack([c, lax.axis_index("kv"), chip]).astype(jnp.int32)

    cache = pack(cache_keys, cache_values)
    own = pack(incoming_keys, new_values)
    near = jnp.concatenate([cache, own], axis=0)
    near_pair = swap(near)
    other, mate = near_pair[:16], near_pair[16:]

    w_both, w_half = weight_pack(info, comp_key_weight.T, comp_value_weight)
    sides = [(2 * k, 2 * ((k + 1) % 4)) for k in range(4)]
    sides += [(2 * k + 1, 2 * ((k - 1) % 4) + 1) for k in range(4)]
    w1_mine = lax.ppermute(w_both, ("kv", "c"), sides)
    w2_mine = lax.ppermute(w_half, "kv", [(k, (k + 2) % 4) for k in range(4)])
    w1_other = swap(w1_mine)
    w2_other = swap(w2_mine)

    chosen = select_blocks.reshape(-1)
    shard, local = chosen >> 4, chosen & 15
    zs, ys, cs = shard >> 3, (shard >> 1) & 3, shard & 1
    n = chosen.shape[0]
    before = jnp.arange(n)[None, :] < jnp.arange(n)[:, None]
    order = jnp.sum(((shard[:, None] == shard[None, :]) & before).astype(jnp.int32), axis=1)
    delta = (z - zs) & 7
    up = (delta >= 1) & (delta <= 3)
    down = delta >= 5
    relay_core = jnp.where(up, 0, jnp.where(down, 1, cs))
    source = jnp.where(
        up,
        2 * delta - 1 + cs,
        jnp.where(down, 2 * (8 - delta) - 1 + (1 - cs), jnp.where(delta == 4, 7, 0)),
    )
    relay, slot = ys * 2 + relay_core, source * 2 + order
    flat = relay * 16 + slot
    request = jnp.sum(
        jnp.where(flat[None, :] == jnp.arange(128, dtype=jnp.int32)[:, None], local[None, :], 0),
        axis=1,
    ).reshape(Y * C, 16)
    rq = lax.all_to_all(request, ("y", "c"), split_axis=0, concat_axis=0, tiled=True)
    rq = jnp.clip(rq, 0, 15)
    chunk = jnp.zeros_like(slot)
    index = relay * 6 + slot
    for k, (low, high) in enumerate(((6, 10), (10, 16))):
        inside = slot >= low
        chunk = jnp.where(inside, k + 1, chunk)
        index = jnp.where(inside, relay * (high - low) + slot - low, index)

    tail = jnp.where(c == 1, cache[8:16], other[8:16])
    last = chip == Z * Y - 1
    before1 = jnp.where(c == 0, tail[4:8], jnp.concatenate([tail[6:8], tail[4:6]]))
    ship = jnp.where(last, before1, jnp.concatenate([own, mate]))
    ship = jnp.concatenate([ship, other[15:16]])
    chips = Z * Y
    pairs = [(2 * q, 2 * ((q + 1) % chips)) for q in range(chips)]
    pairs += [(2 * q + 1, 2 * (q + 2) + 1) for q in range(chips - 2)]
    pairs += [(2 * (chips - 1) + 1, 3)]
    got = lax.ppermute(ship, ("z", "y", "c"), pairs)
    far = jnp.concatenate([tail[2:4], tail[0:2]])
    far = lax.ppermute(far, ("z", "y", "c"), [(2 * (chips - 1) + k, k) for k in range(2)])

    ring = [(2 * k, 2 * ((k + 1) % Z)) for k in range(Z)]
    ring += [(2 * k + 1, 2 * ((k - 1) % Z) + 1) for k in range(Z)]
    pair = jnp.concatenate([cache, other], axis=0)
    steps = [pair]
    for k in range(1, 5):
        x = steps[-1] if k < 4 else steps[-1][:16]
        steps.append(lax.ppermute(x, ("z", "c"), ring))
    _, r1, r2, r3, r4 = steps

    def exchange(srcs, plan, first, loaded=()):
        sent = gather_blocks(srcs, plan, first, rq, loaded)
        return lax.all_to_all(sent, ("y", "c"), split_axis=0, concat_axis=0, tiled=True)

    twice = ((0, 0), (0, 0), (0, 16), (0, 16))
    after = tuple((1, base) for _, base in twice)
    gots = (
        exchange((cache, r1), twice[:2] + after, 0, (1,)),
        exchange((r2,), twice, 6),
        exchange((r3, r4), twice + after[:2], 10),
    )

    qa, qb, g = query_layout(queries, gate_weight.transpose(2, 0, 1))
    t = queries.shape[0]
    wt = swap(got)
    acc = by_heads(
        functools.partial(window_kernel, coef), (info,),
        (qa, qb, g, got, wt, far, jnp.concatenate([own, mate])), (), 768, F32,
        [pltpu.VMEM((4, ROWS, 128), BF)] * 2 + [pltpu.VMEM((2, t, 384), F32)]
        + score_scratch(HB * t, 768),
    )

    xk = cache_keys.reshape(-1, 16 * key_width)
    xv = cache_values.reshape(-1, 16 * cache_values.shape[1])
    comp = compress(
        info, xk, xv, near_pair, got, w_both, w1_mine, w2_mine, w1_other, w2_other,
    )
    column = [comp]
    for k in range(1, 4):
        column.append(lax.ppermute(comp, "y", [(i, (i + k) % Y) for i in range(Y)]))
    column = lax.optimization_barrier(jnp.concatenate(column))
    plane = jnp.concatenate([column, swap(column)])
    by_two = [(2 * k, 2 * ((k + 2) % Z)) for k in range(Z)]
    by_two += [(2 * k + 1, 2 * ((k - 2) % Z) + 1) for k in range(Z)]
    one = lax.ppermute(plane, ("z", "c"), ring)
    two = lax.ppermute(plane, ("z", "c"), by_two)
    three = lax.ppermute(one, ("z", "c"), by_two)
    four = lax.ppermute(two[:4], ("z", "c"), by_two)
    mine = (one, two, three, four)
    turned = []
    for part in mine:
        turned.append(swap(part))
    away = jnp.where(z <= 4, z, 8 - z) - 1
    carrier = jnp.where(z <= 4, 0, 1)
    hole = jnp.stack(
        [
            jnp.where(z == 0, 0, jnp.where(carrier == c, 1, 5) + away),
            jnp.where(z == 0, y + 4 * c, y + 4 * carrier),
        ]
    ).astype(jnp.int32)
    acc = by_heads(
        functools.partial(compressed_kernel, coef), (hole,),
        (qa, qb, g, acc, plane, *mine, *turned), (), 4096, F32,
        score_scratch(HB * t, 4096),
    )
    return by_heads(
        functools.partial(selected_kernel, coef), (chunk, index),
        (qa, qb, g, acc), gots, 1024, BF,
        [pltpu.VMEM((n, ROWS, 128), BF), pltpu.SemaphoreType.DMA((n,))]
        + score_scratch(heads * t // TILES, 1024),
    )


def solution(mesh):
    wide = Mesh(mesh.devices.reshape(4, Z, Y, C), ("kv", "z", "y", "c"))
    seq = ("z", "y", "c")
    placed = (
        P(seq, "kv"),
        P(seq, "kv"),
        P(seq, "kv"),
        P(seq, "kv"),
        P(seq, "kv"),
        P("kv", None),
        P("kv", None),
        P(seq, "kv", None),
        P("kv", None, None),
    )
    return jax.shard_map(
        shards, mesh=wide, in_specs=placed, out_specs=P(seq, "kv"), check_vma=False
    )
```

```python
import functools
import math

import jax
import jax.numpy as jnp
from jax import lax
from jax.experimental import pallas as pl
from jax.experimental.pallas import tpu as pltpu
from jax.sharding import Mesh, PartitionSpec as P


BLOCK = 64
ROWS = 160
WINDOW = 512
MASKED = -1e30
BF = jnp.bfloat16
F32 = jnp.float32
Z, Y, C = 8, 4, 2


def limit(mib):
    return pltpu.CompilerParams(vmem_limit_bytes=mib << 20)


def pack(keys, values):
    k = keys.reshape(-1, BLOCK, keys.shape[1])
    v = values.reshape(-1, BLOCK, values.shape[1])
    high = jnp.concatenate([k[:, :32, 128:], k[:, 32:, 128:]], axis=2)
    return jnp.concatenate([v, k[:, :, :128], high], axis=1)


def nt_dot(a, b):
    return lax.dot_general(a, b, (((1,), (1,)), ((), ())), preferred_element_type=F32)


def stage(n, coef, score, value, ahead, now, finish):
    peak = acc = None
    at = 0
    for j in range(n):
        v = value(0 if now is None else now[0], j)
        w = v.shape[0]
        if ahead is not None:
            g, s_ref, m_ref = ahead
            s = score(g, j)
            s_ref[:, at : at + w] = s
            for k in range(0, w, 128):
                piece = s[:, k : k + 128]
                peak = piece if peak is None else jnp.maximum(peak, piece)
        if now is not None:
            g, s_ref, m_ref = now
            top = m_ref[...]
            p = [
                jnp.exp2(s_ref[:, k : k + 128] * coef - top).astype(BF)
                for k in range(at, at + w, 128)
            ]
            both = jnp.concatenate([v, jnp.ones_like(v)], axis=1)
            part = jnp.dot(jnp.concatenate(p, axis=1), both, preferred_element_type=F32)
            acc = part if acc is None else acc + part
        at += w
    if ahead is not None:
        m_ref = ahead[2]
        peak = jnp.max(peak, axis=1, keepdims=True) * coef
        m_ref[...] = jnp.broadcast_to(peak, m_ref.shape)
    if now is not None:
        finish(now[0], acc[:, :128] / acc[:, 128:])


def attend_groups(groups, n, coef, score, value, finish, ready, refs):
    sa, sb, ma, mb = refs
    ready(0)
    stage(n, coef, score, value, (0, sa, ma), None, finish)

    def body(i, carry):
        ready(2 * i + 1)
        stage(n, coef, score, value, (2 * i + 1, sb, mb), (2 * i, sa, ma), finish)

        @pl.when(2 * i + 2 < groups)
        def _():
            ready(2 * i + 2)
            stage(n, coef, score, value, (2 * i + 2, sa, ma), (2 * i + 1, sb, mb), finish)

        @pl.when(2 * i + 2 >= groups)
        def _():
            stage(n, coef, score, value, None, (2 * i + 1, sb, mb), finish)

        return carry

    lax.fori_loop(0, groups // 2, body, 0)


def score_scratch(rows, keys):
    return [pltpu.VMEM((rows, keys), F32)] * 2 + [pltpu.VMEM((rows, 128), F32)] * 2


def query_kernel(q_ref, g_ref, qa_ref, qb_ref, gate_ref):
    heads = qa_ref.shape[0]
    gates = jnp.concatenate([g_ref[b] for b in range(3)], axis=0)
    for h in range(heads):
        x = q_ref[:, 192 * h : 192 * h + 192]
        zero = jnp.zeros((x.shape[0], 64), BF)
        qa = jnp.concatenate([x, zero], axis=1)
        qa_ref[h] = qa
        qb_ref[h] = jnp.concatenate([x[:, :128], zero, x[:, 128:]], axis=1)
        logits = nt_dot(x, gates)
        for b in range(3):
            at = b * heads + h
            gate_ref[h, :, b : b + 1] = jax.nn.sigmoid(logits[:, at : at + 1])


def query_layout(queries, g):
    heads, t = g.shape[1], queries.shape[0]
    shape = jax.ShapeDtypeStruct((heads, t, 256), BF)
    return pl.pallas_call(
        query_kernel,
        out_shape=(shape, shape, jax.ShapeDtypeStruct((heads, t, 8), F32)),
        cost_estimate=pl.CostEstimate(flops=0, bytes_accessed=4 << 20, transcendentals=0),
        name="query_layout",
    )(queries, g)


def gather_kernel(plan, first, rq, *refs):
    srcs, out_ref, sem = refs[:-2], refs[-2], refs[-1]
    width = len(plan)
    copies = []
    for dest in range(Y * C):
        for s, (src, base) in enumerate(plan):
            i = dest * width + s
            copy = pltpu.make_async_copy(
                srcs[src].at[base + rq[dest, first + s]], out_ref.at[i], sem.at[i]
            )
            copy.start()
            copies.append(copy)
    for copy in copies:
        copy.wait()


def gather_blocks(srcs, plan, first, rq, loaded=()):
    specs = [pl.BlockSpec(memory_space=pl.ANY)] * len(srcs)
    for k in loaded:
        specs[k] = pl.BlockSpec(srcs[k].shape, lambda i, rq: (0, 0, 0))
    count = Y * C * len(plan)
    return pl.pallas_call(
        functools.partial(gather_kernel, plan, first),
        grid_spec=pltpu.PrefetchScalarGridSpec(
            num_scalar_prefetch=1,
            grid=(1,),
            in_specs=specs,
            out_specs=pl.BlockSpec(memory_space=pltpu.HBM),
            scratch_shapes=[pltpu.SemaphoreType.DMA((count,))],
        ),
        out_shape=jax.ShapeDtypeStruct((count, ROWS, 128), BF),
        cost_estimate=pl.CostEstimate(
            flops=0, bytes_accessed=count * ROWS * 128 * 4, transcendentals=0
        ),
        compiler_params=limit(4),
        name="gather_blocks",
    )(rq, *srcs)


def weight_kernel(info, k_ref, v_ref, both_ref, half_ref):
    c = info[0]
    for h in range(2):
        for j in range(6):
            x = k_ref[:, 768 * h + 128 * j : 768 * h + 128 * j + 128]
            both_ref[h, 192 * j : 192 * j + 192, :] = x
        both_ref[h, 1152:1664, :] = v_ref[512 * h : 512 * h + 512, :]
    half_ref[...] = both_ref[c]


def weight_pack(info, wk, wv):
    whole = lambda a: pl.BlockSpec(a.shape, lambda i, c: (0, 0))
    return pl.pallas_call(
        weight_kernel,
        grid_spec=pltpu.PrefetchScalarGridSpec(
            num_scalar_prefetch=1,
            grid=(1,),
            in_specs=[whole(wk), whole(wv)],
            out_specs=(
                pl.BlockSpec((2, 1664, 128), lambda i, c: (0, 0, 0)),
                pl.BlockSpec((1664, 128), lambda i, c: (0, 0)),
            ),
        ),
        out_shape=(
            jax.ShapeDtypeStruct((2, 1664, 128), BF),
            jax.ShapeDtypeStruct((1664, 128), BF),
        ),
        cost_estimate=pl.CostEstimate(flops=0, bytes_accessed=3 << 20, transcendentals=0),
        name="weight_pack",
    )(info, wk, wv)


def compress_kernel(
    info, xk_ref, xv_ref, ea_ref, eb_ref, own_ref, m1_ref, m2_ref, o1_ref, o2_ref, out_ref,
    ek_ref, ev_ref,
):
    c, x = info[0], info[1]
    edge = jnp.where(c == 1, ea_ref[0].astype(F32), eb_ref[0].astype(F32))
    ev_ref[...] = edge[48:64]
    ek_ref[...] = jnp.concatenate([edge[112:128], edge[144:160, 64:128]], axis=1)
    row = lax.broadcasted_iota(jnp.int32, (64, 1), 0)

    def taken(ref, edge, at, width, first):
        a = ref[:, pl.ds(pl.multiple_of(at * width, 256), 4 * width)].astype(F32)
        before = jnp.concatenate([edge[pl.ds(at + k, 1), :] for k in range(4)], axis=1)
        lead = jnp.where(row == 0, before, jnp.roll(a, 1, axis=0))
        return jnp.where(first, lead, a).astype(BF)

    step = 1 - 2 * c
    near, far, across = (x - step) & 3, (x + step) & 3, (x + 2) & 3
    pieces = [(own_ref.at[h], x, h) for h in range(2)]
    pieces += [(m1_ref.at[h], near, h) for h in range(2)]
    pieces += [(o1_ref.at[h], far, h) for h in range(2)]
    pieces += [(m2_ref, across, c), (o2_ref, across, 1 - c)]
    keys = jnp.zeros((64, 192), F32)
    values = jnp.zeros((64, 128), F32)
    for ref, i, h in pieces:
        at = 8 * (i & 1) + 4 * h
        a = taken(xk_ref, ek_ref, at, 192, i < 2)
        for j in range(3):
            w = jnp.concatenate(
                [ref[384 * j : 384 * j + 192, :], ref[384 * j + 192 : 384 * j + 384, :]], axis=1
            )
            keys = keys + nt_dot(a[:, 256 * j : 256 * j + 256], w)
        a = taken(xv_ref, ev_ref, at, 128, i < 2)
        values = values + jnp.dot(a, ref[1152:1664, :], preferred_element_type=F32)
    keys = keys.astype(BF)
    out_ref[0, 0:64, :] = values.astype(BF)
    out_ref[0, 64:128, :] = keys[:, :128]
    out_ref[0, 128:160, :] = jnp.concatenate([keys[:32, 128:], keys[32:, 128:]], axis=1)


def compress(info, *args):
    full = lambda a: pl.BlockSpec(a.shape, lambda i, c, n=a.ndim: (0,) * n)
    return pl.pallas_call(
        compress_kernel,
        grid_spec=pltpu.PrefetchScalarGridSpec(
            num_scalar_prefetch=1,
            grid=(1,),
            in_specs=[full(a) for a in args[:2]]
            + [pl.BlockSpec((1, ROWS, 128), lambda i, c, k=k: (k, 0, 0)) for k in (15, 4)]
            + [full(a) for a in args[4:]],
            out_specs=pl.BlockSpec((1, ROWS, 128), lambda i, c: (0, 0, 0)),
            scratch_shapes=[pltpu.VMEM((16, 192), F32), pltpu.VMEM((16, 128), F32)],
        ),
        out_shape=jax.ShapeDtypeStruct((1, ROWS, 128), BF),
        cost_estimate=pl.CostEstimate(
            flops=2 * 64 * (6144 * 192 + 4096 * 128), bytes_accessed=4 << 20, transcendentals=0
        ),
        name="compress",
    )(info, *args)


HB = 4


def part_of(ref, first, count, part):
    n = count * 32
    blocks = pl.ds(first, count)
    low = ref[blocks, 64 + 32 * part : 96 + 32 * part, :].reshape(n, 128)
    high = ref[blocks, 128:160, :].reshape(n, 128)
    return jnp.concatenate([low, high], axis=1)


def values_of(ref, first, count, part):
    return ref[pl.ds(first, count), 32 * part : 32 * part + 32, :].reshape(count * 32, 128)


def nothing(g):
    pass


def window_kernel(
    coef, info, qa_ref, qb_ref, g_ref, got_ref, turned_ref, far_ref, own_ref, out_ref,
    wm_ref, wt_ref, bias, *refs
):
    c = info[0]
    first = info[2] == 0
    wm_ref[...] = jnp.where(first & (c == 1), far_ref[...], got_ref[0:4])
    wt_ref[...] = jnp.where(first & (c == 0), far_ref[...], turned_ref[0:4])
    t = qa_ref.shape[1]
    rows = HB * t
    plan = ((wm_ref, -256 - 256 * c, c), (wt_ref, -512 + 256 * c, 1 - c), (own_ref, 0, c))
    at = lax.broadcasted_iota(jnp.int32, (t, 1), 0) + c * t
    for part in range(2):
        for k, (ref, base, ring) in enumerate(plan):
            i = lax.broadcasted_iota(jnp.int32, (1, 128), 1)
            which = lax.shift_right_logical(i, 6)
            which = which + ring - 2 * which * ring
            where = base + which * t + (lax.shift_right_logical(i, 5) & 1) * 64 + part * 32
            where = where + (i & 31)
            ok = (where <= at) & (where > at - WINDOW)
            bias[part, :, 128 * k : 128 * k + 128] = jnp.where(ok, 0.0, MASKED)

    def score(g, j):
        q = (qa_ref, qb_ref)[j][pl.ds(g * HB, HB)].reshape(rows, 256)
        k = jnp.concatenate([part_of(ref, 0, 4, j) for ref, _, _ in plan], axis=0)
        s = nt_dot(q, k).reshape(HB, t, 384) + bias[j][None]
        return s.reshape(rows, 384)

    def value(g, j):
        return jnp.concatenate([values_of(ref, 0, 4, j) for ref, _, _ in plan], axis=0)

    def finish(g, out):
        for h in range(HB):
            sl = pl.ds(pl.multiple_of((g * HB + h) * 128, 128), 128)
            out_ref[:, sl] = out[h * t : (h + 1) * t] * g_ref[g * HB + h, :, 2:3]

    attend_groups(qa_ref.shape[0] // HB, 2, coef, score, value, finish, nothing, refs)


def compressed_kernel(
    coef, hole, qa_ref, qb_ref, g_ref, add_ref, *refs
):
    blocks, out_ref, refs = refs[:9], refs[9], refs[10:]
    t = qa_ref.shape[1]
    rows = HB * t
    plan = [
        (kinds, part) for kinds in ((0, 4, 8), (1, 2), (3, 5), (6, 7)) for part in range(2)
    ]

    def score(g, j):
        kinds, part = plan[j]
        q = (qa_ref, qb_ref)[part][pl.ds(g * HB, HB)].reshape(rows, 256)
        keys = [part_of(blocks[k], 0, blocks[k].shape[0], part) for k in kinds]
        s = nt_dot(q, jnp.concatenate(keys, axis=0))
        if part == 0:
            at = jnp.int32(-1)
            start = 0
            for k in kinds:
                at = jnp.where(hole[0] == k, start + hole[1] * 32, at)
                start += blocks[k].shape[0] * 32
            col = lax.broadcasted_iota(jnp.int32, (1, start), 1)
            s = jnp.where(col == at, MASKED, s)
        return s

    def value(g, j):
        kinds, part = plan[j]
        v = [values_of(blocks[k], 0, blocks[k].shape[0], part) for k in kinds]
        return jnp.concatenate(v, axis=0)

    def finish(g, out):
        for h in range(HB):
            sl = pl.ds(pl.multiple_of((g * HB + h) * 128, 128), 128)
            gated = out[h * t : (h + 1) * t] * g_ref[g * HB + h, :, 0:1]
            out_ref[:, sl] = add_ref[:, sl] + gated

    attend_groups(qa_ref.shape[0] // HB, len(plan), coef, score, value, finish, nothing, refs)


TILES = 4


def selected_kernel(coef, chunk, index, *refs):
    sources, gots, out_ref, buf, sem = refs[:4], refs[4:7], refs[7], refs[8], refs[9]
    qa_ref, qb_ref, g_ref, add_ref = refs[10:14]
    loads = [
        pltpu.make_async_copy(src, dst, refs[14].at[k])
        for k, (src, dst) in enumerate(zip(sources, refs[10:14]))
    ]
    for load in loads:
        load.start()
    heads = qa_ref.shape[0]
    t = qa_ref.shape[1] // TILES
    rows = heads * t
    per = buf.shape[0] // TILES

    def fetch(n, carry):
        for k in range(3):
            @pl.when(chunk[n] == k)
            def _():
                pltpu.make_async_copy(gots[k].at[index[n]], buf.at[n], sem.at[n]).start()

        return carry

    lax.fori_loop(0, buf.shape[0], fetch, 0)
    for load in loads:
        load.wait()

    def ready(g):
        def wait(j, carry):
            n = g * per + j
            pltpu.make_async_copy(gots[0].at[0], buf.at[n], sem.at[n]).wait()
            return carry

        lax.fori_loop(0, per, wait, 0)

    def tile(g):
        return pl.ds(pl.multiple_of(g * t, t), t)

    def score(g, j):
        q = (qa_ref, qb_ref)[j][:, tile(g), :].reshape(rows, 256)
        return nt_dot(q, part_of(buf, g * per, per, j))

    def value(g, j):
        return values_of(buf, g * per, per, j)

    def finish(g, out):
        for h in range(heads):
            hs = slice(128 * h, 128 * h + 128)
            gated = out[h * t : (h + 1) * t] * g_ref[h, tile(g), 1:2]
            out_ref[tile(g), hs] = (add_ref[tile(g), hs] + gated).astype(BF)

    attend_groups(TILES, 2, coef, score, value, finish, ready, refs[15:])


def cost(rows, keys):
    return pl.CostEstimate(
        flops=2 * rows * keys * 512, bytes_accessed=6 << 20, transcendentals=rows * keys
    )


def by_heads(kernel, scalars, args, moved, keys, dtype, scratch):
    heads, t, _ = (args + moved)[0].shape
    whole = lambda a: pl.BlockSpec(a.shape, lambda i, *_, n=a.ndim: (0,) * n)
    return pl.pallas_call(
        kernel,
        grid_spec=pltpu.PrefetchScalarGridSpec(
            num_scalar_prefetch=len(scalars),
            grid=(1,),
            in_specs=[whole(a) for a in args] + [pl.BlockSpec(memory_space=pl.ANY) for _ in moved],
            out_specs=pl.BlockSpec((t, heads * 128), lambda i, *_: (0, 0)),
            scratch_shapes=scratch,
        ),
        out_shape=jax.ShapeDtypeStruct((t, heads * 128), dtype),
        cost_estimate=cost(heads * t, keys),
    )(*scalars, *args, *moved)


def swap(x):
    return lax.ppermute(x, "c", [(0, 1), (1, 0)])


def shards(
    queries,
    cache_keys,
    cache_values,
    incoming_keys,
    new_values,
    comp_key_weight,
    comp_value_weight,
    select_blocks,
    gate_weight,
):
    heads, key_width, _ = gate_weight.shape
    coef = key_width ** (-0.5) * math.log2(math.e)
    z, y, c = lax.axis_index("z"), lax.axis_index("y"), lax.axis_index("c")
    chip = z * Y + y
    info = jnp.stack([c, lax.axis_index("kv"), chip]).astype(jnp.int32)

    cache = pack(cache_keys, cache_values)
    own = pack(incoming_keys, new_values)
    near = jnp.concatenate([cache, own], axis=0)
    near_pair = swap(near)
    other, mate = near_pair[:16], near_pair[16:]

    w_both, w_half = weight_pack(info, comp_key_weight.T, comp_value_weight)
    sides = [(2 * k, 2 * ((k + 1) % 4)) for k in range(4)]
    sides += [(2 * k + 1, 2 * ((k - 1) % 4) + 1) for k in range(4)]
    w1_mine = lax.ppermute(w_both, ("kv", "c"), sides)
    w2_mine = lax.ppermute(w_half, "kv", [(k, (k + 2) % 4) for k in range(4)])
    w1_other = swap(w1_mine)
    w2_other = swap(w2_mine)

    chosen = select_blocks.reshape(-1)
    shard, local = chosen >> 4, chosen & 15
    zs, ys, cs = shard >> 3, (shard >> 1) & 3, shard & 1
    n = chosen.shape[0]
    before = jnp.arange(n)[None, :] < jnp.arange(n)[:, None]
    order = jnp.sum(((shard[:, None] == shard[None, :]) & before).astype(jnp.int32), axis=1)
    delta = (z - zs) & 7
    up = (delta >= 1) & (delta <= 3)
    down = delta >= 5
    relay_core = jnp.where(up, 0, jnp.where(down, 1, cs))
    source = jnp.where(
        up,
        2 * delta - 1 + cs,
        jnp.where(down, 2 * (8 - delta) - 1 + (1 - cs), jnp.where(delta == 4, 7, 0)),
    )
    relay, slot = ys * 2 + relay_core, source * 2 + order
    flat = relay * 16 + slot
    request = jnp.sum(
        jnp.where(flat[None, :] == jnp.arange(128, dtype=jnp.int32)[:, None], local[None, :], 0),
        axis=1,
    ).reshape(Y * C, 16)
    rq = lax.all_to_all(request, ("y", "c"), split_axis=0, concat_axis=0, tiled=True)
    rq = jnp.clip(rq, 0, 15)
    chunk = jnp.zeros_like(slot)
    index = relay * 6 + slot
    for k, (low, high) in enumerate(((6, 10), (10, 16))):
        inside = slot >= low
        chunk = jnp.where(inside, k + 1, chunk)
        index = jnp.where(inside, relay * (high - low) + slot - low, index)

    tail = jnp.where(c == 1, cache[8:16], other[8:16])
    last = chip == Z * Y - 1
    before1 = jnp.where(c == 0, tail[4:8], jnp.concatenate([tail[6:8], tail[4:6]]))
    ship = jnp.where(last, before1, jnp.concatenate([own, mate]))
    ship = jnp.concatenate([ship, other[15:16]])
    chips = Z * Y
    pairs = [(2 * q, 2 * ((q + 1) % chips)) for q in range(chips)]
    pairs += [(2 * q + 1, 2 * (q + 2) + 1) for q in range(chips - 2)]
    pairs += [(2 * (chips - 1) + 1, 3)]
    got = lax.ppermute(ship, ("z", "y", "c"), pairs)
    far = jnp.concatenate([tail[2:4], tail[0:2]])
    far = lax.ppermute(far, ("z", "y", "c"), [(2 * (chips - 1) + k, k) for k in range(2)])

    ring = [(2 * k, 2 * ((k + 1) % Z)) for k in range(Z)]
    ring += [(2 * k + 1, 2 * ((k - 1) % Z) + 1) for k in range(Z)]
    pair = jnp.concatenate([cache, other], axis=0)
    steps = [pair]
    for k in range(1, 5):
        x = steps[-1] if k < 4 else steps[-1][:16]
        steps.append(lax.ppermute(x, ("z", "c"), ring))
    _, r1, r2, r3, r4 = steps

    def exchange(srcs, plan, first, loaded=()):
        sent = gather_blocks(srcs, plan, first, rq, loaded)
        return lax.all_to_all(sent, ("y", "c"), split_axis=0, concat_axis=0, tiled=True)

    twice = ((0, 0), (0, 0), (0, 16), (0, 16))
    after = tuple((1, base) for _, base in twice)
    gots = (
        exchange((cache, r1), twice[:2] + after, 0),
        exchange((r2,), twice, 6),
        exchange((r3, r4), twice + after[:2], 10),
    )

    qa, qb, g = query_layout(queries, gate_weight.transpose(2, 0, 1))
    t = queries.shape[0]
    wt = swap(got)
    acc = by_heads(
        functools.partial(window_kernel, coef), (info,),
        (qa, qb, g, got, wt, far, jnp.concatenate([own, mate])), (), 768, F32,
        [pltpu.VMEM((4, ROWS, 128), BF)] * 2 + [pltpu.VMEM((2, t, 384), F32)]
        + score_scratch(HB * t, 768),
    )

    xk = cache_keys.reshape(-1, 16 * key_width)
    xv = cache_values.reshape(-1, 16 * cache_values.shape[1])
    comp = compress(
        info, xk, xv, near_pair, got, w_both, w1_mine, w2_mine, w1_other, w2_other,
    )
    column = [comp]
    for k in range(1, 4):
        column.append(lax.ppermute(comp, "y", [(i, (i + k) % Y) for i in range(Y)]))
    column = lax.optimization_barrier(jnp.concatenate(column))
    plane = jnp.concatenate([column, swap(column)])
    by_two = [(2 * k, 2 * ((k + 2) % Z)) for k in range(Z)]
    by_two += [(2 * k + 1, 2 * ((k - 2) % Z) + 1) for k in range(Z)]
    one = lax.ppermute(plane, ("z", "c"), ring)
    two = lax.ppermute(plane, ("z", "c"), by_two)
    three = lax.ppermute(one, ("z", "c"), by_two)
    four = lax.ppermute(two[:4], ("z", "c"), by_two)
    mine = (one, two, three, four)
    turned = []
    for part in mine:
        turned.append(swap(part))
    away = jnp.where(z <= 4, z, 8 - z) - 1
    carrier = jnp.where(z <= 4, 0, 1)
    hole = jnp.stack(
        [
            jnp.where(z == 0, 0, jnp.where(carrier == c, 1, 5) + away),
            jnp.where(z == 0, y + 4 * c, y + 4 * carrier),
        ]
    ).astype(jnp.int32)
    acc = by_heads(
        functools.partial(compressed_kernel, coef), (hole,),
        (qa, qb, g, acc, plane, *mine, *turned), (), 4096, F32,
        score_scratch(HB * t, 4096),
    )
    return by_heads(
        functools.partial(selected_kernel, coef), (chunk, index),
        (), (qa, qb, g, acc) + gots, 1024, BF,
        [pltpu.VMEM((n, ROWS, 128), BF), pltpu.SemaphoreType.DMA((n,))]
        + [pltpu.VMEM(a.shape, a.dtype) for a in (qa, qb, g, acc)]
        + [pltpu.SemaphoreType.DMA((4,))]
        + score_scratch(heads * t // TILES, 1024),
    )


def solution(mesh):
    wide = Mesh(mesh.devices.reshape(4, Z, Y, C), ("kv", "z", "y", "c"))
    seq = ("z", "y", "c")
    placed = (
        P(seq, "kv"),
        P(seq, "kv"),
        P(seq, "kv"),
        P(seq, "kv"),
        P(seq, "kv"),
        P("kv", None),
        P("kv", None),
        P(seq, "kv", None),
        P("kv", None, None),
    )
    return jax.shard_map(
        shards, mesh=wide, in_specs=placed, out_specs=P(seq, "kv"), check_vma=False
    )
```
